32 devices in a mesh: groups: 2 (over y), rows: 4 (over z), cols: 4 (over x, core).
Axes of the slice: x: 2, y: 2, z: 4, core: 2. Of those that a mesh axis runs over, the one named last changes fastest.
Arguments:
- tokens: bfloat16 [128, 256, 512], P(('groups', 'rows'), 'cols'), parts along dimension 0, may hold values from -30 to 30
- qkv_weight: bfloat16 [512, 1536], replicated, may hold values from -0.25 to 0.25
- depth_kernel: float32 [25, 1536], replicated, may hold values from -1.25 to 1.25
- group_kernel: bfloat16 [48, 32, 32], replicated, may hold values from -1 to 1
- proj_weight: bfloat16 [1024, 512], replicated, may hold values from -0.1875 to 0.1875
- out_gain: float32 [512], replicated, may hold values from 4 to 16
- out_bias: float32 [512], replicated, may hold values from -3 to 3
Outputs:
- output: bfloat16 [128, 256, 512], P(('groups', 'rows'), 'cols'), parts along dimension 0
The draws below stay inside these ranges and needn't reach their ends.
There are 2 independent parts, one for each index of `groups`. The reference program is written for one: setup_inputs(seed, part) draws one part's arguments, and reference() takes and returns one part's arrays. A program takes and returns all parts, laid end to end along the dimension named above; an argument that names none is the same for every part. Nothing has to cross between parts.
All inputs are finite; a program needn't handle non-finite values.
Results may differ from the reference program's by a relative error of at most 0.0048.
Values may be sent and summed in bfloat16 or wider, within the bound.
A program may use at most 64 MiB of HBM per device.

```python
import math
import jax
import jax.numpy as jnp
from jax import lax

D = 512
HEAD_DIM = 32
HEADS = 16
TILE_ROWS = 16
HEIGHT = 64
WIDTH = 256
N_ROWS = 4


def draw_tokens(key, part):
    parts_keys = jax.random.split(key, 3)
    region_rows = HEIGHT // 4 + 1
    region_cols = WIDTH // 4 + 1
    region = jax.random.normal(parts_keys[0], (region_rows, region_cols, D), jnp.float32)
    region_scale = jnp.exp(jax.random.uniform(parts_keys[1], (region_rows, region_cols), jnp.float32, math.log(0.5), math.log(2.0)))
    row_of = jnp.arange(HEIGHT) // 4
    col_of = jnp.arange(WIDTH) // 4
    base = (region * region_scale[:, :, None])[row_of][:, col_of]
    rising = 1.0 + 2.0 * jnp.arange(HEIGHT, dtype=jnp.float32) / max(HEIGHT - 1, 1)
    noise = jax.random.normal(parts_keys[2], (HEIGHT, WIDTH, D), jnp.float32)
    field = 0.8 * base + 0.6 * noise
    return jnp.clip(field * rising[:, None, None], -30.0, 30.0).astype(jnp.bfloat16)


def bell_draw(key, dims, deviation, bound, kind=jnp.bfloat16):
    array = jax.random.normal(key, dims, jnp.float32) * deviation
    return jnp.minimum(jnp.maximum(array, -bound), bound).astype(kind)


def setup_inputs(seed: int = 0, part: int = 0) -> dict:
    keys = jax.random.split(jax.random.key(seed), 8)
    part_keys = jax.random.split(jax.random.fold_in(keys[7], part), 8)
    tokens = draw_tokens(jax.random.fold_in(jax.random.fold_in(keys[7], part), 71), part)
    qkv_weight = bell_draw(keys[1], (D, 3 * D), D ** -0.5, 0.25)
    depth_kernel = bell_draw(keys[2], (25, 3 * D), 25 ** -0.5, 1.25, jnp.float32)
    group_kernel = bell_draw(keys[3], (3 * HEADS, HEAD_DIM, HEAD_DIM), HEAD_DIM ** -0.5, 1.0)
    proj_weight = bell_draw(keys[4], (2 * D, D), (2 * D) ** -0.5, 0.1875)
    out_gain = jnp.clip(jnp.exp(jax.random.uniform(keys[5], (D,), jnp.float32, math.log(4.0), math.log(16.0))), 4.0, 16.0)
    out_bias = bell_draw(keys[6], (D,), 0.5, 3.0, jnp.float32)
    return dict(tokens=tokens, qkv_weight=qkv_weight, depth_kernel=depth_kernel, group_kernel=group_kernel, proj_weight=proj_weight, out_gain=out_gain, out_bias=out_bias)


def feature_map(inputs):
    return jax.nn.elu(inputs.astype(jnp.float32)) + 1.0


def aggregate(padded, depth_kernel, group_kernel, height, breadth):
    channels = padded.shape[2]
    summed = jnp.zeros((height, breadth, channels), jnp.float32)
    for offset_row in range(5):
        for offset_col in range(5):
            window = padded[offset_row:offset_row + height, offset_col:offset_col + breadth].astype(jnp.float32)
            summed = summed + window * depth_kernel[offset_row * 5 + offset_col]
    spread = summed.astype(jnp.bfloat16).reshape(height * breadth, channels // HEAD_DIM, HEAD_DIM)
    grouped = jnp.einsum("ngc,gcd->ngd", spread.astype(jnp.float32), group_kernel.astype(jnp.float32))
    return grouped.astype(jnp.bfloat16).reshape(height, breadth, channels)


def context_states(source):
    amount = source.shape[0]
    grouped = source.reshape(amount, -1, 3, HEAD_DIM)
    key_feats = feature_map(grouped[:, :, 1]).astype(jnp.bfloat16).astype(jnp.float32)
    values = grouped[:, :, 2].astype(jnp.float32)
    states = jnp.einsum("nhd,nhe->hde", key_feats, values)
    totals = jnp.sum(key_feats, axis=0)
    return states, totals


def reference(tokens, qkv_weight, depth_kernel, group_kernel, proj_weight, out_gain, out_bias):
    triple = jnp.dot(tokens.reshape(HEIGHT * WIDTH, D), qkv_weight, preferred_element_type=jnp.float32)
    triple = triple.astype(jnp.bfloat16).reshape(HEIGHT, WIDTH, 3 * D)
    padded = jnp.pad(triple, ((2, 2), (2, 2), (0, 0)))
    band_ids = jnp.arange(N_ROWS, dtype=jnp.int32)

    def band_aggregate(index):
        rows_in = lax.dynamic_slice_in_dim(padded, index * TILE_ROWS, TILE_ROWS + 4, 0)
        return aggregate(rows_in, depth_kernel, group_kernel, TILE_ROWS, WIDTH)

    aggregated = lax.map(band_aggregate, band_ids).reshape(HEIGHT, WIDTH, 3 * D)

    def band_pair(index):
        plain = lax.dynamic_slice_in_dim(triple, index * TILE_ROWS, TILE_ROWS, 0).reshape(-1, 3 * D)
        scaled = lax.dynamic_slice_in_dim(aggregated, index * TILE_ROWS, TILE_ROWS, 0).reshape(-1, 3 * D)
        return plain, scaled

    def band_states(index):
        plain, scaled = band_pair(index)
        plain_state, plain_total = context_states(plain)
        scaled_state, scaled_total = context_states(scaled)
        return jnp.concatenate([plain_state, scaled_state], 0), jnp.concatenate([plain_total, scaled_total], 0)

    band_s, band_z = lax.map(band_states, band_ids)
    states = jnp.sum(band_s, axis=0)
    totals = jnp.sum(band_z, axis=0)

    def band_output(index):
        plain, scaled = band_pair(index)
        amount = plain.shape[0]
        queries = jnp.concatenate([
            feature_map(plain.reshape(amount, -1, 3, HEAD_DIM)[:, :, 0]),
            feature_map(scaled.reshape(amount, -1, 3, HEAD_DIM)[:, :, 0])], 1)
        numerator = jnp.einsum("nhd,hde->nhe", queries, states, precision=lax.Precision.HIGHEST)
        denominator = jnp.einsum("nhd,hd->nh", queries, totals, precision=lax.Precision.HIGHEST)
        attended = (numerator / denominator[:, :, None]).astype(jnp.bfloat16).reshape(amount, 2 * D)
        projected = jnp.dot(attended, proj_weight, preferred_element_type=jnp.float32)
        source = lax.dynamic_slice_in_dim(tokens, index * TILE_ROWS, TILE_ROWS, 0).reshape(amount, D)
        result = source.astype(jnp.float32) + out_gain * projected + out_bias
        return result.astype(jnp.bfloat16)

    output = lax.map(band_output, band_ids)
    return output.reshape(HEIGHT, WIDTH, D)
```

```python
import functools

import jax
import jax.numpy as jnp
from jax import lax
from jax.experimental import pallas as pl
from jax.experimental.pallas import tpu as pltpu
from jax.sharding import PartitionSpec as P

HEAD_DIM = 32
PACK = 8 * HEAD_DIM
LANES = 128
SUB = 16
PAD = 8
LINES = 4
BF = jnp.bfloat16
F32 = jnp.float32
ROLL = jnp.bfloat16
WAYS = ((1, 0), (-1, 0), (0, 1), (0, -1), (1, 1), (1, -1), (-1, 1), (-1, -1))


def iota(shape, dim):
    return lax.broadcasted_iota(jnp.int32, shape, dim)


def dot(a, b):
    return jnp.dot(a, b, preferred_element_type=F32)


def feature_map(u):
    return jnp.where(u > 0, u + 1.0, jnp.exp(jnp.minimum(u, 0.0)))


def one_hot(mask):
    return jnp.where(mask, 1.0, 0.0).astype(BF)


def kernel(
    n_rows, n_cols,
    tok_ref, w_ref, dk_ref, gk_ref, pw_ref, gain_ref, bias_ref,
    out_ref,
    stage_e, stage_c, halo_e, halo_c, halo_r, wq, taps, gsq, gbd, stag, spread, acc, mix,
    part, rs, ar_src, ar, ag,
    halo_send, halo_recv, red_send, red_recv,
):
    height, breadth, d = tok_ref.shape
    inner = breadth // SUB
    wide = inner + 4
    amount = height * breadth
    n_pack = d // PACK
    n_chunk = d // LANES
    pitch = breadth + 2 * PAD
    mr, mc = lax.axis_index("rows"), lax.axis_index("cols")

    def exists(way):
        r, c = mr + way[0], mc + way[1]
        return (r >= 0) & (r < n_rows) & (c >= 0) & (c < n_cols)

    def at(r, c):
        return {"rows": r, "cols": c}

    MESH = pl.DeviceIdType.MESH
    barrier = pltpu.get_barrier_semaphore()
    for k in range(1, n_rows):
        pl.semaphore_signal(barrier, inc=1, device_id=at(lax.rem(mr + k, n_rows), mc), device_id_type=MESH)
    for k in range(1, n_cols):
        pl.semaphore_signal(barrier, inc=1, device_id=at(mr, lax.rem(mc + k, n_cols)), device_id_type=MESH)
    for way in WAYS[4:]:
        @pl.when(exists(way))
        def _():
            pl.semaphore_signal(barrier, inc=1, device_id=at(mr + way[0], mc + way[1]), device_id_type=MESH)

    e = 2 * height
    rows_out = 2 * e + 4 * SUB
    m = iota((rows_out, amount), 0)
    src = iota((rows_out, amount), 1)
    right = (m >= e).astype(jnp.int32)
    me_ = m - right * e
    edge = (me_ % height) * breadth + me_ // height + right * (breadth - 2)
    cm = m - 2 * e
    ci, cr = cm // SUB, cm % SUB
    corner = ((cr % 2) + (ci // 2) * (height - 2)) * breadth + (cr // 2) + (ci % 2) * (breadth - 2)
    want = jnp.where(m < 2 * e, edge, jnp.where(cr < 4, corner, -1))
    sel = dot(one_hot(want == src), tok_ref[...].reshape(amount, d)).astype(BF)
    stage_e[...] = sel[: 2 * e].reshape(2, e, d)
    stage_c[...] = sel[2 * e :].reshape(4, SUB, d)

    moves = (
        (tok_ref.at[pl.ds(height - 2, 2)], halo_r.at[0]),
        (tok_ref.at[pl.ds(0, 2)], halo_r.at[1]),
        (stage_e.at[1], halo_e.at[0]),
        (stage_e.at[0], halo_e.at[1]),
        (stage_c.at[3], halo_c.at[0]),
        (stage_c.at[2], halo_c.at[1]),
        (stage_c.at[1], halo_c.at[2]),
        (stage_c.at[0], halo_c.at[3]),
    )

    def halo_copy(i):
        way = WAYS[i]
        return pltpu.make_async_remote_copy(
            src_ref=moves[i][0], dst_ref=moves[i][1],
            send_sem=halo_send.at[i], recv_sem=halo_recv.at[i],
            device_id=at(mr + way[0], mc + way[1]), device_id_type=MESH,
        )

    def regroup(x, y, z):
        quarter = iota(x.shape, 1) // HEAD_DIM
        x64, z64 = pltpu.roll(x, 64, 1), pltpu.roll(z, 64, 1)

        def choose(a, b, c, e):
            return jnp.where(quarter < 2, jnp.where(quarter == 0, a, b), jnp.where(quarter == 2, c, e))

        return (
            choose(x, x64, y, z64),
            choose(pltpu.roll(x, 96, 1), pltpu.roll(y, 32, 1), pltpu.roll(y, 96, 1), pltpu.roll(z, 32, 1)),
            choose(x64, y, z64, z),
        )

    for i in range(n_chunk):
        native = [w_ref[:, (3 * i + t) * LANES : (3 * i + t + 1) * LANES].astype(ROLL) for t in range(3)]
        for t, tile in enumerate(regroup(*native)):
            wq[:, t * d + i * LANES : t * d + (i + 1) * LANES] = tile.astype(BF)

    def put(ch, row, block):
        stag[ch, pl.ds(row * pitch + PAD, breadth), :] = block

    tokens = tok_ref[...].reshape(amount, d)

    def project(first, last):
        for p in range(first, last):
            y = dot(tokens, wq[:, p * PACK : (p + 1) * PACK])
            for c in range(PACK // LANES):
                for r in range(height):
                    put(2 * p + c, r + 2, y[r * breadth : (r + 1) * breadth, c * LANES : (c + 1) * LANES])

    project(n_pack, 3 * n_pack)

    n_diag = sum(exists(way).astype(jnp.int32) for way in WAYS[4:])
    pl.semaphore_wait(barrier, n_rows - 1 + n_cols - 1 + n_diag)
    for i, way in enumerate(WAYS):
        @pl.when(exists(way))
        def _():
            halo_copy(i).start()

        @pl.when(jnp.logical_not(exists((-way[0], -way[1]))))
        def _():
            dst = moves[i][1]
            dst[...] = jnp.zeros(dst.shape, BF)

    project(0, n_pack)

    prow, pcol = iota((PACK, PACK), 0), iota((PACK, PACK), 1)
    same = prow // HEAD_DIM == pcol // HEAD_DIM
    same_hot = one_hot(same)
    dn = (((0,), (0,)), ((), ()))

    def local_states(z, get_k, get_v):
        pieces, totals = [], []
        for i in range(n_pack):
            k = feature_map(get_k(i))
            totals.append(jnp.sum(k, axis=0, keepdims=True))
            st = lax.dot_general(k.astype(BF), get_v(i).astype(BF), dn, preferred_element_type=F32)
            pieces.append(jnp.sum(jnp.where(same, st, 0.0).reshape(8, HEAD_DIM, PACK), axis=0))
        line = jnp.concatenate(totals, axis=1)
        spot = iota((HEAD_DIM, LANES), 0)
        total = jnp.zeros((HEAD_DIM, LANES), F32)
        for i in range(n_chunk):
            total = jnp.where(spot == i, line[:, i * LANES : (i + 1) * LANES], total)
        flat = jnp.concatenate(pieces + [total], axis=1)
        step = HEAD_DIM // n_cols
        for q in range(n_cols):
            part[z, q] = flat[q * step : (q + 1) * step]

    def rs_copy(z, k):
        peer = lax.rem(mc + k, n_cols)
        return pltpu.make_async_remote_copy(
            src_ref=part.at[z, peer], dst_ref=rs.at[z, k - 1],
            send_sem=red_send.at[z, 0, k - 1], recv_sem=red_recv.at[z, 0, k - 1],
            device_id=at(mr, peer), device_id_type=MESH,
        )

    def ar_copy(z, k):
        return pltpu.make_async_remote_copy(
            src_ref=ar_src.at[z], dst_ref=ar.at[z, k - 1],
            send_sem=red_send.at[z, 1, k - 1], recv_sem=red_recv.at[z, 1, k - 1],
            device_id=at(lax.rem(mr + k, n_rows), mc), device_id_type=MESH,
        )

    def ag_copy(z, k):
        return pltpu.make_async_remote_copy(
            src_ref=ag.at[z, mc], dst_ref=ag.at[z, mc],
            send_sem=red_send.at[z, 2, k - 1], recv_sem=red_recv.at[z, 2, k - 1],
            device_id=at(mr, lax.rem(mc + k, n_cols)), device_id_type=MESH,
        )

    def ag_wait(z, k):
        sender = lax.rem(mc - k + n_cols, n_cols)
        pltpu.make_async_remote_copy(
            src_ref=ag.at[z, mc], dst_ref=ag.at[z, sender],
            send_sem=red_send.at[z, 2, k - 1], recv_sem=red_recv.at[z, 2, k - 1],
            device_id=at(mr, sender), device_id_type=MESH,
        ).wait_recv()

    def reduce_1(z):
        for k in range(1, n_cols):
            rs_copy(z, k).start()

    def reduce_2(z):
        total = part[z, mc]
        for k in range(1, n_cols):
            rs_copy(z, k).wait_recv()
            total = total + rs[z, k - 1]
        ar_src[z] = total
        for k in range(1, n_rows):
            ar_copy(z, k).start()

    def reduce_3(z):
        total = ar_src[z]
        for k in range(1, n_rows):
            ar_copy(z, k).wait_recv()
            total = total + ar[z, k - 1]
        ag[z, mc] = total
        for k in range(1, n_cols):
            ag_copy(z, k).start()

    def reduce_4(z):
        for k in range(1, n_cols):
            ag_wait(z, k)
        return jnp.concatenate([ag[z, q] for q in range(n_cols)], axis=0)

    def conv(first, last):
        def chunk(ch, _):
            w = [jnp.broadcast_to(taps[ch, t : t + 1, :], (SUB, LANES)).astype(BF) for t in range(25)]

            def lines(q, _):
                r0 = q * LINES
                sums = [[None] * inner for _ in range(LINES)]
                for rr in range(LINES + 4):
                    start = (r0 + rr) * pitch + PAD - 2
                    xs = [stag[ch, pl.ds(start + jj, SUB, stride=inner), :].astype(BF) for jj in range(wide)]
                    for n in range(LINES):
                        a = rr - n
                        if 0 <= a < 5:
                            for j in range(inner):
                                term = xs[j] * w[5 * a]
                                for b in range(1, 5):
                                    term = term + xs[j + b] * w[5 * a + b]
                                sums[n][j] = term if a == 0 else sums[n][j] + term
                for n in range(LINES):
                    for j in range(inner):
                        spread[ch, pl.ds((r0 + n) * breadth + j, SUB, stride=inner), :] = sums[n][j].astype(F32)
                return 0

            lax.fori_loop(0, height // LINES, lines, 0)
            return 0

        lax.fori_loop(first, last, chunk, 0)

    def native(t, i):
        lo = (t * d + i * PACK) // LANES
        return jnp.concatenate(
            [
                jnp.concatenate([stag[lo + c, pl.ds((r + 2) * pitch + PAD, breadth), :] for r in range(height)], axis=0)
                for c in range(PACK // LANES)
            ],
            axis=1,
        )

    def grouped(t, i):
        lo = (t * d + i * PACK) // LANES
        x = jnp.concatenate([spread[lo + c].astype(BF) for c in range(PACK // LANES)], axis=1)
        return dot(x, gbd[t * n_pack + i])

    def attend(z, flat, get_q):
        qs, dens = [], []
        for i in range(n_pack):
            rows = slice(z * d + i * PACK, z * d + (i + 1) * PACK)
            st = flat[:, i * PACK : (i + 1) * PACK]
            st = jnp.where(same, jnp.concatenate([st] * 8, axis=0), 0.0).astype(BF)
            mix[i * PACK : (i + 1) * PACK, :] = (dot(st, pw_ref[rows, :]) * gain_ref[...]).astype(BF)
        heads = []
        for i in range(n_pack):
            tot = jnp.concatenate([flat[2 * i + c : 2 * i + c + 1, d:] for c in range(PACK // LANES)], axis=1)
            q = feature_map(get_q(i))
            den = dot((q * tot).astype(BF), same_hot)
            heads.append((q * pl.reciprocal(den, approx=True)).astype(BF))
        return dot(jnp.concatenate(heads, axis=1), mix[...])

    local_states(0, lambda i: native(1, i), lambda i: native(2, i))
    reduce_1(0)
    for i in range(n_chunk):
        native_taps = [dk_ref[:, (3 * i + t) * LANES : (3 * i + t + 1) * LANES] for t in range(3)]
        for t, tile in enumerate(regroup(*native_taps)):
            taps[t * n_chunk + i, :25, :] = tile

    n_group = gk_ref.shape[2]
    eye = one_hot(iota((n_group, n_group), 0) == iota((n_group, n_group), 1))
    flat_gk = gk_ref[...].reshape(HEAD_DIM * HEAD_DIM, n_group)
    turned = lax.dot_general(eye, flat_gk, (((1,), (1,)), ((), ())), preferred_element_type=F32)
    quarter = iota((n_group, LANES), 1) // HEAD_DIM
    for k in range(HEAD_DIM * HEAD_DIM // LANES):
        tile = turned[:, k * LANES : (k + 1) * LANES]
        turns = [tile] + [pltpu.roll(tile, n * HEAD_DIM, 1) for n in range(1, 4)]
        for j in range(4):
            t0, t1, t2, t3 = (turns[(b - j) % 4] for b in range(4))
            copy = jnp.where(quarter < 2, jnp.where(quarter == 0, t0, t1), jnp.where(quarter == 2, t2, t3))
            gsq[pl.ds(4 * k + j, n_group, stride=HEAD_DIM), :] = copy
    own = iota((LANES, LANES), 0) // HEAD_DIM == iota((LANES, LANES), 1) // HEAD_DIM
    blank = jnp.zeros((LANES, LANES), BF)
    for t in range(3):
        for i in range(n_pack):
            blocks = []
            for c in range(PACK // LANES):
                base = 4 * (2 * i + c)
                block = jnp.concatenate(
                    [gsq[(3 * (base + h) + t) * HEAD_DIM : (3 * (base + h) + t + 1) * HEAD_DIM, :] for h in range(4)], axis=0)
                blocks.append(jnp.where(own, block, 0.0).astype(BF))
            gbd[t * n_pack + i, :LANES, :] = jnp.concatenate([blocks[0], blank], axis=1)
            gbd[t * n_pack + i, LANES:, :] = jnp.concatenate([blank, blocks[1]], axis=1)

    for i, way in enumerate(WAYS):
        @pl.when(exists((-way[0], -way[1])))
        def _():
            halo_copy(i).wait_recv()

    around = jnp.concatenate(
        [halo_r[...].reshape(4 * breadth, d), halo_e[...].reshape(2 * e, d), halo_c[...].reshape(4 * SUB, d)], axis=0)
    for p in range(3 * n_pack):
        y = dot(around, wq[:, p * PACK : (p + 1) * PACK])
        for c in range(PACK // LANES):
            ch = 2 * p + c
            cut = y[:, c * LANES : (c + 1) * LANES]
            for n, row in enumerate((0, 1, height + 2, height + 3)):
                put(ch, row, cut[n * breadth : (n + 1) * breadth])
            for side in range(2):
                for b in range(2):
                    col = (breadth + PAD if side else PAD - 2) + b
                    lo = 4 * breadth + side * e + b * height
                    stag[ch, pl.ds(2 * pitch + col, height, stride=pitch), :] = cut[lo : lo + height]
                    for n in range(2):
                        lo = 4 * breadth + 2 * e + (2 * n + side) * SUB + 2 * b
                        row = n * (height + 2)
                        stag[ch, pl.ds(row * pitch + col, 2, stride=pitch), :] = cut[lo : lo + 2]

    conv(n_chunk, 2 * n_chunk)
    reduce_2(0)
    conv(2 * n_chunk, 3 * n_chunk)
    reduce_3(0)
    local_states(1, lambda i: grouped(1, i), lambda i: grouped(2, i))
    reduce_1(1)
    conv(0, n_chunk // 2)
    reduce_2(1)
    conv(n_chunk // 2, n_chunk)
    reduce_3(1)
    acc[...] = attend(0, reduce_4(0), lambda i: native(0, i)) + (tokens.astype(F32) + bias_ref[...])
    got = acc[...] + attend(1, reduce_4(1), lambda i: grouped(0, i))
    out_ref[...] = got.astype(BF).reshape(height, breadth, d)

    for i, way in enumerate(WAYS):
        @pl.when(exists(way))
        def _():
            halo_copy(i).wait_send()
    for z in range(2):
        for k in range(1, n_cols):
            rs_copy(z, k).wait_send()
            ag_copy(z, k).wait_send()
        for k in range(1, n_rows):
            ar_copy(z, k).wait_send()


def body(n_rows, n_cols, tokens, qkv_weight, depth_kernel, group_kernel, proj_weight, out_gain, out_bias):
    height, breadth, d = tokens.shape
    step = HEAD_DIM // n_cols
    msg = d + LANES
    most = max(n_rows, n_cols)
    vmem = pl.BlockSpec(memory_space=pltpu.VMEM)
    return pl.pallas_call(
        functools.partial(kernel, n_rows, n_cols),
        out_shape=jax.ShapeDtypeStruct((height, breadth, d), BF),
        in_specs=[vmem] * 7,
        out_specs=vmem,
        scratch_shapes=[
            pltpu.VMEM((2, 2 * height, d), BF),
            pltpu.VMEM((4, SUB, d), BF),
            pltpu.VMEM((2, 2 * height, d), BF),
            pltpu.VMEM((4, SUB, d), BF),
            pltpu.VMEM((2, 2, breadth, d), BF),
            pltpu.VMEM((d, 3 * d), BF),
            pltpu.VMEM((3 * d // LANES, 32, LANES), F32),
            pltpu.VMEM((3 * d, LANES), F32),
            pltpu.VMEM((3 * d // PACK, PACK, PACK), BF),
            pltpu.VMEM((3 * d // LANES, (height + 4) * (breadth + 2 * PAD), LANES), F32),
            pltpu.VMEM((3 * d // LANES, height * breadth, LANES), F32),
            pltpu.VMEM((height * breadth, d), F32),
            pltpu.VMEM((d, d), BF),
            pltpu.VMEM((2, n_cols, step, msg), F32),
            pltpu.VMEM((2, n_cols - 1, step, msg), F32),
            pltpu.VMEM((2, step, msg), F32),
            pltpu.VMEM((2, n_rows - 1, step, msg), F32),
            pltpu.VMEM((2, n_cols, step, msg), F32),
            pltpu.SemaphoreType.DMA((8,)),
            pltpu.SemaphoreType.DMA((8,)),
            pltpu.SemaphoreType.DMA((2, 3, most)),
            pltpu.SemaphoreType.DMA((2, 3, most)),
        ],
        compiler_params=pltpu.CompilerParams(
            collective_id=0, has_side_effects=True, vmem_limit_bytes=56 * 1024 * 1024
        ),
        name="attention_module",
    )(tokens, qkv_weight, depth_kernel, jnp.transpose(group_kernel, (1, 2, 0)), proj_weight, out_gain[None, :], out_bias[None, :])


def solution(mesh):
    placed = (P(("groups", "rows"), "cols", None), P(), P(), P(), P(), P(), P())
    return jax.shard_map(
        functools.partial(body, mesh.shape["rows"], mesh.shape["cols"]),
        mesh=mesh,
        in_specs=placed,
        out_specs=P(("groups", "rows"), "cols", None),
        check_vma=False,
    )
```

```python
import functools

import jax
import jax.numpy as jnp
from jax import lax
from jax.experimental import pallas as pl
from jax.experimental.pallas import tpu as pltpu
from jax.sharding import PartitionSpec as P

HEAD_DIM = 32
PACK = 8 * HEAD_DIM
LANES = 128
SUB = 16
PAD = 8
LINES = 4
BF = jnp.bfloat16
F32 = jnp.float32
WAYS = ((1, 0), (-1, 0), (0, 1), (0, -1), (1, 1), (1, -1), (-1, 1), (-1, -1))


def iota(shape, dim):
    return lax.broadcasted_iota(jnp.int32, shape, dim)


def dot(a, b):
    return jnp.dot(a, b, preferred_element_type=F32)


def feature_map(u):
    return jnp.where(u > 0, u + 1.0, jnp.exp(jnp.minimum(u, 0.0)))


def one_hot(mask):
    return jnp.where(mask, 1.0, 0.0).astype(BF)


def kernel(
    n_rows, n_cols,
    *refs,
):
    sources, out_ref, refs = refs[:7], refs[7], refs[8:]
    inputs, refs = refs[:7], refs[7:]
    tok_ref, w_ref, dk_ref, gk_ref, pw_ref, gain_ref, bias_ref = inputs
    (
    stage_e, stage_c, halo_e, halo_c, halo_r, wq, taps, gsq, gbd, stag, spread, acc, mix, result,
    part, rs, ar_src, ar, ag,
    halo_send, halo_recv, red_send, red_recv, load, done,
    ) = refs

    def fetch(i):
        return pltpu.make_async_copy(sources[i], inputs[i], load.at[i])

    for i in range(7):
        fetch(i).start()
    height, breadth, d = tok_ref.shape
    inner = breadth // SUB
    wide = inner + 4
    amount = height * breadth
    n_pack = d // PACK
    n_chunk = d // LANES
    pitch = breadth + 2 * PAD
    mr, mc = lax.axis_index("rows"), lax.axis_index("cols")

    def exists(way):
        r, c = mr + way[0], mc + way[1]
        return (r >= 0) & (r < n_rows) & (c >= 0) & (c < n_cols)

    def at(r, c):
        return {"rows": r, "cols": c}

    MESH = pl.DeviceIdType.MESH
    barrier = pltpu.get_barrier_semaphore()
    n_all = n_rows * n_cols
    direct = HEAD_DIM % n_all == 0
    me = mr * n_cols + mc
    if direct:
        for k in range(1, n_all):
            peer = lax.rem(me + k, n_all)
            pl.semaphore_signal(
                barrier, inc=1, device_id=at(peer // n_cols, lax.rem(peer, n_cols)), device_id_type=MESH)
    else:
        for k in range(1, n_rows):
            pl.semaphore_signal(barrier, inc=1, device_id=at(lax.rem(mr + k, n_rows), mc), device_id_type=MESH)
        for k in range(1, n_cols):
            pl.semaphore_signal(barrier, inc=1, device_id=at(mr, lax.rem(mc + k, n_cols)), device_id_type=MESH)
        for way in WAYS[4:]:
            @pl.when(exists(way))
            def _():
                pl.semaphore_signal(barrier, inc=1, device_id=at(mr + way[0], mc + way[1]), device_id_type=MESH)

    fetch(0).wait()
    e = 2 * height
    rows_out = 2 * e + 4 * SUB
    m = iota((rows_out, amount), 0)
    src = iota((rows_out, amount), 1)
    right = (m >= e).astype(jnp.int32)
    me_ = m - right * e
    edge = (me_ % height) * breadth + me_ // height + right * (breadth - 2)
    cm = m - 2 * e
    ci, cr = cm // SUB, cm % SUB
    corner = ((cr % 2) + (ci // 2) * (height - 2)) * breadth + (cr // 2) + (ci % 2) * (breadth - 2)
    want = jnp.where(m < 2 * e, edge, jnp.where(cr < 4, corner, -1))
    sel = dot(one_hot(want == src), tok_ref[...].reshape(amount, d)).astype(BF)
    stage_e[...] = sel[: 2 * e].reshape(2, e, d)
    stage_c[...] = sel[2 * e :].reshape(4, SUB, d)

    moves = (
        (tok_ref.at[pl.ds(height - 2, 2)], halo_r.at[0]),
        (tok_ref.at[pl.ds(0, 2)], halo_r.at[1]),
        (stage_e.at[1], halo_e.at[0]),
        (stage_e.at[0], halo_e.at[1]),
        (stage_c.at[3], halo_c.at[0]),
        (stage_c.at[2], halo_c.at[1]),
        (stage_c.at[1], halo_c.at[2]),
        (stage_c.at[0], halo_c.at[3]),
    )

    def halo_copy(i):
        way = WAYS[i]
        return pltpu.make_async_remote_copy(
            src_ref=moves[i][0], dst_ref=moves[i][1],
            send_sem=halo_send.at[i], recv_sem=halo_recv.at[i],
            device_id=at(mr + way[0], mc + way[1]), device_id_type=MESH,
        )

    def regroup(x, y, z, kinds):
        quarter = iota(x.shape, 1) // HEAD_DIM
        def choose(a, b, c, e):
            return jnp.where(quarter < 2, jnp.where(quarter == 0, a, b), jnp.where(quarter == 2, c, e))

        def turn(a, n):
            return pltpu.roll(a, n * HEAD_DIM, 1)

        makers = (
            lambda: choose(x, turn(x, 2), y, turn(z, 2)),
            lambda: choose(turn(x, 3), turn(y, 1), turn(y, 3), turn(z, 1)),
            lambda: choose(turn(x, 2), y, turn(z, 2), z),
        )
        return [(t, makers[t]()) for t in kinds]

    def order_weights(kinds):
        for i in range(n_chunk):
            native = [w_ref[:, (3 * i + t) * LANES : (3 * i + t + 1) * LANES] for t in range(3)]
            for t, tile in regroup(*native, kinds):
                wq[:, t * d + i * LANES : t * d + (i + 1) * LANES] = tile

    def put(ch, row, block):
        stag[ch, pl.ds(row * pitch + PAD, breadth), :] = block

    tokens = tok_ref[...].reshape(amount, d)

    def project(first, last):
        for p in range(first, last):
            y = dot(tokens, wq[:, p * PACK : (p + 1) * PACK])
            for c in range(PACK // LANES):
                for r in range(height):
                    put(2 * p + c, r + 2, y[r * breadth : (r + 1) * breadth, c * LANES : (c + 1) * LANES])

    fetch(1).wait()
    order_weights((1, 2))
    project(n_pack, 3 * n_pack)

    if direct:
        pl.semaphore_wait(barrier, n_all - 1)
    else:
        n_diag = sum(exists(way).astype(jnp.int32) for way in WAYS[4:])
        pl.semaphore_wait(barrier, n_rows - 1 + n_cols - 1 + n_diag)
    for i, way in enumerate(WAYS):
        @pl.when(exists(way))
        def _():
            halo_copy(i).start()

        @pl.when(jnp.logical_not(exists((-way[0], -way[1]))))
        def _():
            dst = moves[i][1]
            dst[...] = jnp.zeros(dst.shape, BF)


    prow, pcol = iota((PACK, PACK), 0), iota((PACK, PACK), 1)
    same = prow // HEAD_DIM == pcol // HEAD_DIM
    same_hot = one_hot(same)
    dn = (((0,), (0,)), ((), ()))

    def local_states(z, get_k, get_v):
        pieces, totals = [], []
        for i in range(n_pack):
            k = feature_map(get_k(i))
            totals.append(jnp.sum(k, axis=0, keepdims=True))
            st = lax.dot_general(k.astype(BF), get_v(i).astype(BF), dn, preferred_element_type=F32)
            pieces.append(jnp.sum(jnp.where(same, st, 0.0).reshape(8, HEAD_DIM, PACK), axis=0))
        line = jnp.concatenate(totals, axis=1)
        spot = iota((HEAD_DIM, LANES), 0)
        total = jnp.zeros((HEAD_DIM, LANES), F32)
        for i in range(n_chunk):
            total = jnp.where(spot == i, line[:, i * LANES : (i + 1) * LANES], total)
        flat = jnp.concatenate(pieces + [total], axis=1)
        step = HEAD_DIM // ways
        for q in range(ways):
            part[z, q] = flat[q * step : (q + 1) * step]

    def rs_copy(z, k):
        if direct:
            peer = lax.rem(me + k, n_all)
            device = at(peer // n_cols, lax.rem(peer, n_cols))
        else:
            peer = lax.rem(mc + k, n_cols)
            device = at(mr, peer)
        return pltpu.make_async_remote_copy(
            src_ref=part.at[z, peer], dst_ref=rs.at[z, k - 1],
            send_sem=red_send.at[z, 0, k - 1], recv_sem=red_recv.at[z, 0, k - 1],
            device_id=device, device_id_type=MESH,
        )

    def ar_copy(z, k):
        return pltpu.make_async_remote_copy(
            src_ref=ar_src.at[z], dst_ref=ar.at[z, k - 1],
            send_sem=red_send.at[z, 1, k - 1], recv_sem=red_recv.at[z, 1, k - 1],
            device_id=at(lax.rem(mr + k, n_rows), mc), device_id_type=MESH,
        )

    ways = n_all if direct else n_cols
    slot = me if direct else mc

    def ag_copy(z, k, back=False):
        peer = lax.rem(slot + (ways - k if back else k), ways)
        device = at(peer // n_cols, lax.rem(peer, n_cols)) if direct else at(mr, peer)
        return pltpu.make_async_remote_copy(
            src_ref=ag.at[z, slot], dst_ref=ag.at[z, peer if back else slot],
            send_sem=red_send.at[z, 2, k - 1], recv_sem=red_recv.at[z, 2, k - 1],
            device_id=device, device_id_type=MESH,
        )

    def gather(z, total):
        ag[z, slot] = total
        for k in range(1, ways):
            ag_copy(z, k).start()

    def reduce_1(z):
        for k in range(1, ways):
            rs_copy(z, k).start()

    def reduce_2(z):
        total = part[z, slot]
        for k in range(1, ways):
            rs_copy(z, k).wait_recv()
            total = total + rs[z, k - 1]
        if direct:
            gather(z, total)
            return
        ar_src[z] = total
        for k in range(1, n_rows):
            ar_copy(z, k).start()

    def reduce_3(z):
        if direct:
            return
        total = ar_src[z]
        for k in range(1, n_rows):
            ar_copy(z, k).wait_recv()
            total = total + ar[z, k - 1]
        gather(z, total)

    def reduce_4(z):
        for k in range(1, ways):
            ag_copy(z, k, back=True).wait_recv()
        return jnp.concatenate([ag[z, q] for q in range(ways)], axis=0)

    def conv(first, last, start_row, n_lines, hop, count):
        def chunk(ch, _):
            w = [jnp.broadcast_to(taps[ch, t : t + 1, :], (SUB, LANES)).astype(BF) for t in range(25)]

            def lines(q, _):
                r0 = start_row + q * hop
                sums = [[None] * inner for _ in range(n_lines)]
                for rr in range(n_lines + 4):
                    start = (r0 + rr) * pitch + PAD - 2
                    xs = [stag[ch, pl.ds(start + jj, SUB, stride=inner), :].astype(BF) for jj in range(wide)]
                    for n in range(n_lines):
                        a = rr - n
                        if 0 <= a < 5:
                            for j in range(inner):
                                term = xs[j] * w[5 * a]
                                for b in range(1, 5):
                                    term = term + xs[j + b] * w[5 * a + b]
                                sums[n][j] = term if a == 0 else sums[n][j] + term
                for n in range(n_lines):
                    for j in range(inner):
                        spread[ch, pl.ds((r0 + n) * breadth + j, SUB, stride=inner), :] = sums[n][j].astype(F32)
                return 0

            lax.fori_loop(0, count, lines, 0)
            return 0

        lax.fori_loop(first, last, chunk, 0)

    def native(t, i):
        lo = (t * d + i * PACK) // LANES
        return jnp.concatenate(
            [
                jnp.concatenate([stag[lo + c, pl.ds((r + 2) * pitch + PAD, breadth), :] for r in range(height)], axis=0)
                for c in range(PACK // LANES)
            ],
            axis=1,
        )

    def grouped(t, i):
        lo = (t * d + i * PACK) // LANES
        x = jnp.concatenate([spread[lo + c].astype(BF) for c in range(PACK // LANES)], axis=1)
        return dot(x, gbd[t * n_pack + i])

    def mix_states(z, flat):
        for i in range(n_pack):
            rows = slice(z * d + i * PACK, z * d + (i + 1) * PACK)
            st = flat[:, i * PACK : (i + 1) * PACK]
            st = jnp.where(same, jnp.concatenate([st] * 8, axis=0), 0.0).astype(BF)
            mix[i * PACK : (i + 1) * PACK, :] = (dot(st, pw_ref[rows, :]) * gain_ref[...]).astype(BF)

    def attend(flat, get_q):
        heads = []
        for i in range(n_pack):
            tot = jnp.concatenate([flat[2 * i + c : 2 * i + c + 1, d:] for c in range(PACK // LANES)], axis=1)
            q = get_q(i)
            den = dot((q * tot).astype(BF), same_hot)
            heads.append((q * pl.reciprocal(den, approx=True)).astype(BF))
        return dot(jnp.concatenate(heads, axis=1), mix[...])

    local_states(0, lambda i: native(1, i), lambda i: native(2, i))
    reduce_1(0)
    fetch(2).wait()
    for i in range(n_chunk):
        native_taps = [dk_ref[:, (3 * i + t) * LANES : (3 * i + t + 1) * LANES] for t in range(3)]
        for t, tile in regroup(*native_taps, (0, 1, 2)):
            taps[t * n_chunk + i, :25, :] = tile

    fetch(3).wait()
    n_group = gk_ref.shape[2]
    eye = one_hot(iota((n_group, n_group), 0) == iota((n_group, n_group), 1))
    flat_gk = gk_ref[...].reshape(HEAD_DIM * HEAD_DIM, n_group)
    turned = lax.dot_general(eye, flat_gk, (((1,), (1,)), ((), ())), preferred_element_type=F32)
    quarter = iota((n_group, LANES), 1) // HEAD_DIM
    for k in range(HEAD_DIM * HEAD_DIM // LANES):
        tile = turned[:, k * LANES : (k + 1) * LANES]
        turns = [tile] + [pltpu.roll(tile, n * HEAD_DIM, 1) for n in range(1, 4)]
        for j in range(4):
            t0, t1, t2, t3 = (turns[(b - j) % 4] for b in range(4))
            copy = jnp.where(quarter < 2, jnp.where(quarter == 0, t0, t1), jnp.where(quarter == 2, t2, t3))
            gsq[pl.ds(4 * k + j, n_group, stride=HEAD_DIM), :] = copy
    own = iota((LANES, LANES), 0) // HEAD_DIM == iota((LANES, LANES), 1) // HEAD_DIM
    blank = jnp.zeros((LANES, LANES), BF)
    for t in range(3):
        for i in range(n_pack):
            blocks = []
            for c in range(PACK // LANES):
                base = 4 * (2 * i + c)
                block = jnp.concatenate(
                    [gsq[(3 * (base + h) + t) * HEAD_DIM : (3 * (base + h) + t + 1) * HEAD_DIM, :] for h in range(4)], axis=0)
                blocks.append(jnp.where(own, block, 0.0).astype(BF))
            gbd[t * n_pack + i, :LANES, :] = jnp.concatenate([blocks[0], blank], axis=1)
            gbd[t * n_pack + i, LANES:, :] = jnp.concatenate([blank, blocks[1]], axis=1)

    def arrived(which):
        for i in which:
            way = WAYS[i]

            @pl.when(exists((-way[0], -way[1])))
            def _():
                halo_copy(i).wait_recv()

    def project_sides(first, last):
        around = halo_e[...].reshape(2 * e, d)
        for p in range(first, last):
            y = dot(around, wq[:, p * PACK : (p + 1) * PACK])
            for c in range(PACK // LANES):
                for side in range(2):
                    for b in range(2):
                        col = (breadth + PAD if side else PAD - 2) + b
                        lo = side * e + b * height
                        stag[2 * p + c, pl.ds(2 * pitch + col, height, stride=pitch), :] = (
                            y[lo : lo + height, c * LANES : (c + 1) * LANES])

    def project_rows(first, last):
        around = jnp.concatenate([halo_r[...].reshape(4 * breadth, d), halo_c[...].reshape(4 * SUB, d)], axis=0)
        for p in range(first, last):
            y = dot(around, wq[:, p * PACK : (p + 1) * PACK])
            for c in range(PACK // LANES):
                ch = 2 * p + c
                cut = y[:, c * LANES : (c + 1) * LANES]
                for n, row in enumerate((0, 1, height + 2, height + 3)):
                    put(ch, row, cut[n * breadth : (n + 1) * breadth])
                for side in range(2):
                    for b in range(2):
                        col = (breadth + PAD if side else PAD - 2) + b
                        for n in range(2):
                            lo = 4 * breadth + (2 * n + side) * SUB + 2 * b
                            row = n * (height + 2)
                            stag[ch, pl.ds(row * pitch + col, 2, stride=pitch), :] = cut[lo : lo + 2]

    arrived((2, 3))
    project_sides(n_pack, 3 * n_pack)
    conv(n_chunk, 3 * n_chunk, 2, LINES, LINES, (height - 4) // LINES)
    arrived((0, 1, 4, 5, 6, 7))
    project_rows(n_pack, 3 * n_pack)
    reduce_2(0)
    conv(n_chunk, 3 * n_chunk, 0, 2, height - 2, 2)
    reduce_3(0)
    local_states(1, lambda i: grouped(1, i), lambda i: grouped(2, i))
    reduce_1(1)
    order_weights((0,))
    project(0, n_pack)
    project_sides(0, n_pack)
    project_rows(0, n_pack)
    whole = (0, LINES, LINES, height // LINES)
    conv(0, n_chunk // 2, *whole)
    reduce_2(1)
    conv(n_chunk // 2, n_chunk, *whole)
    for i in range(4, 7):
        fetch(i).wait()
    flat = reduce_4(0)
    mix_states(0, flat)
    acc[...] = attend(flat, lambda i: feature_map(native(0, i))) + (tokens.astype(F32) + bias_ref[...])
    reduce_3(1)
    for i in range(n_pack):
        q = feature_map(grouped(0, i))
        for c in range(PACK // LANES):
            spread[2 * i + c] = q[:, c * LANES : (c + 1) * LANES]
    flat = reduce_4(1)
    mix_states(1, flat)
    n_part = 2
    piece = height // n_part

    def store(b):
        rows = pl.ds(b * piece, piece)
        return pltpu.make_async_copy(result.at[rows], out_ref.at[rows], done.at[b])

    for b in range(n_part):
        cut = slice(b * piece * breadth, (b + 1) * piece * breadth)
        late = [
            jnp.concatenate([spread[2 * i + c, cut] for c in range(PACK // LANES)], axis=1) for i in range(n_pack)
        ]
        got = acc[cut] + attend(flat, lambda i: late[i])
        result[b * piece : (b + 1) * piece] = got.astype(BF).reshape(piece, breadth, d)
        store(b).start()
    for b in range(n_part):
        store(b).wait()

    for i, way in enumerate(WAYS):
        @pl.when(exists(way))
        def _():
            halo_copy(i).wait_send()
    for z in range(2):
        for k in range(1, ways):
            rs_copy(z, k).wait_send()
            ag_copy(z, k).wait_send()
        if not direct:
            for k in range(1, n_rows):
                ar_copy(z, k).wait_send()


def body(n_rows, n_cols, tokens, qkv_weight, depth_kernel, group_kernel, proj_weight, out_gain, out_bias):
    height, breadth, d = tokens.shape
    ways = n_rows * n_cols if HEAD_DIM % (n_rows * n_cols) == 0 else n_cols
    step = HEAD_DIM // ways
    msg = d + LANES
    most = max(n_rows, ways)
    operands = (
        tokens, qkv_weight, depth_kernel, jnp.transpose(group_kernel, (1, 2, 0)), proj_weight, out_gain[None, :], out_bias[None, :])
    return pl.pallas_call(
        functools.partial(kernel, n_rows, n_cols),
        out_shape=jax.ShapeDtypeStruct((height, breadth, d), BF),
        in_specs=[pl.BlockSpec(memory_space=pl.ANY)] * 7,
        out_specs=pl.BlockSpec(memory_space=pl.ANY),
        scratch_shapes=[pltpu.VMEM(x.shape, x.dtype) for x in operands] + [
            pltpu.VMEM((2, 2 * height, d), BF),
            pltpu.VMEM((4, SUB, d), BF),
            pltpu.VMEM((2, 2 * height, d), BF),
            pltpu.VMEM((4, SUB, d), BF),
            pltpu.VMEM((2, 2, breadth, d), BF),
            pltpu.VMEM((d, 3 * d), BF),
            pltpu.VMEM((3 * d // LANES, 32, LANES), F32),
            pltpu.VMEM((3 * d, LANES), F32),
            pltpu.VMEM((3 * d // PACK, PACK, PACK), BF),
            pltpu.VMEM((3 * d // LANES, (height + 4) * (breadth + 2 * PAD), LANES), F32),
            pltpu.VMEM((3 * d // LANES, height * breadth, LANES), F32),
            pltpu.VMEM((height * breadth, d), F32),
            pltpu.VMEM((d, d), BF),
            pltpu.VMEM((height, breadth, d), BF),
            pltpu.VMEM((2, ways, step, msg), F32),
            pltpu.VMEM((2, ways - 1, step, msg), F32),
            pltpu.VMEM((2, step, msg), F32),
            pltpu.VMEM((2, n_rows - 1, step, msg), F32),
            pltpu.VMEM((2, ways, step, msg), F32),
            pltpu.SemaphoreType.DMA((8,)),
            pltpu.SemaphoreType.DMA((8,)),
            pltpu.SemaphoreType.DMA((2, 3, most)),
            pltpu.SemaphoreType.DMA((2, 3, most)),
            pltpu.SemaphoreType.DMA((7,)),
            pltpu.SemaphoreType.DMA((2,)),
        ],
        compiler_params=pltpu.CompilerParams(
            collective_id=0, has_side_effects=True, vmem_limit_bytes=56 * 1024 * 1024
        ),
        name="attention_module",
    )(*operands)


def solution(mesh):
    placed = (P(("groups", "rows"), "cols", None), P(), P(), P(), P(), P(), P())
    return jax.shard_map(
        functools.partial(body, mesh.shape["rows"], mesh.shape["cols"]),
        mesh=mesh,
        in_specs=placed,
        out_specs=P(("groups", "rows"), "cols", None),
        check_vma=False,
    )
```

```python
import functools

import jax
import jax.numpy as jnp
from jax import lax
from jax.experimental import pallas as pl
from jax.experimental.pallas import tpu as pltpu
from jax.sharding import PartitionSpec as P

HEAD_DIM = 32
PACK = 8 * HEAD_DIM
LANES = 128
SUB = 16
PAD = 8
LINES = 4
ROWS = HEAD_DIM + SUB
BF = jnp.bfloat16
F32 = jnp.float32
WAYS = ((1, 0), (-1, 0), (0, 1), (0, -1), (1, 1), (1, -1), (-1, 1), (-1, -1))


def is_paired(n_rows, n_cols, d):
    return n_cols % 2 == 0 and n_rows * n_cols <= 32 and d == 2 * PACK


def iota(shape, dim):
    return lax.broadcasted_iota(jnp.int32, shape, dim)


def dot(a, b):
    return jnp.dot(a, b, preferred_element_type=F32)


def feature_map(u):
    return jnp.where(u > 0, u + 1.0, jnp.exp(jnp.minimum(u, 0.0)))


def one_hot(mask):
    return jnp.where(mask, 1.0, 0.0).astype(BF)


def kernel(
    n_rows, n_cols,
    *refs,
):
    sources, out_ref, refs = refs[:7], refs[7], refs[8:]
    inputs, refs = refs[:7], refs[7:]
    tok_ref, w_ref, dk_ref, gk_ref, pw_ref, gain_ref, bias_ref = inputs
    (
    stage_e, stage_c, halo_e, halo_c, halo_r, wq, taps, gsq, gbd, stag, spread, acc, mix, result,
    part, rs, ar_src, ar, ag,
    halo_send, halo_recv, red_send, red_recv, load, done,
    ) = refs

    def fetch(i):
        return pltpu.make_async_copy(sources[i], inputs[i], load.at[i])

    for i in range(7):
        fetch(i).start()
    height, breadth, d = tok_ref.shape
    inner = breadth // SUB
    wide = inner + 4
    amount = height * breadth
    n_pack = d // PACK
    n_chunk = d // LANES
    pitch = breadth + 2 * PAD
    mr, mc = lax.axis_index("rows"), lax.axis_index("cols")

    def exists(way):
        r, c = mr + way[0], mc + way[1]
        return (r >= 0) & (r < n_rows) & (c >= 0) & (c < n_cols)

    def at(r, c):
        return {"rows": r, "cols": c}

    MESH = pl.DeviceIdType.MESH
    barrier = pltpu.get_barrier_semaphore()
    n_all = n_rows * n_cols
    paired = is_paired(n_rows, n_cols, d)
    me = mr * n_cols + mc
    if paired:
        for k in range(1, n_all):
            peer = lax.rem(me + k, n_all)
            pl.semaphore_signal(
                barrier, inc=1, device_id=at(peer // n_cols, lax.rem(peer, n_cols)), device_id_type=MESH)
    else:
        for k in range(1, n_rows):
            pl.semaphore_signal(barrier, inc=1, device_id=at(lax.rem(mr + k, n_rows), mc), device_id_type=MESH)
        for k in range(1, n_cols):
            pl.semaphore_signal(barrier, inc=1, device_id=at(mr, lax.rem(mc + k, n_cols)), device_id_type=MESH)
        for way in WAYS[4:]:
            @pl.when(exists(way))
            def _():
                pl.semaphore_signal(barrier, inc=1, device_id=at(mr + way[0], mc + way[1]), device_id_type=MESH)

    fetch(0).wait()
    e = 2 * height
    rows_out = 2 * e + 4 * SUB
    m = iota((rows_out, amount), 0)
    src = iota((rows_out, amount), 1)
    right = (m >= e).astype(jnp.int32)
    me_ = m - right * e
    edge = (me_ % height) * breadth + me_ // height + right * (breadth - 2)
    cm = m - 2 * e
    ci, cr = cm // SUB, cm % SUB
    corner = ((cr % 2) + (ci // 2) * (height - 2)) * breadth + (cr // 2) + (ci % 2) * (breadth - 2)
    want = jnp.where(m < 2 * e, edge, jnp.where(cr < 4, corner, -1))
    sel = dot(one_hot(want == src), tok_ref[...].reshape(amount, d)).astype(BF)
    stage_e[...] = sel[: 2 * e].reshape(2, e, d)
    stage_c[...] = sel[2 * e :].reshape(4, SUB, d)

    moves = (
        (tok_ref.at[pl.ds(height - 2, 2)], halo_r.at[0]),
        (tok_ref.at[pl.ds(0, 2)], halo_r.at[1]),
        (stage_e.at[1], halo_e.at[0]),
        (stage_e.at[0], halo_e.at[1]),
        (stage_c.at[3], halo_c.at[0]),
        (stage_c.at[2], halo_c.at[1]),
        (stage_c.at[1], halo_c.at[2]),
        (stage_c.at[0], halo_c.at[3]),
    )

    def halo_copy(i):
        way = WAYS[i]
        return pltpu.make_async_remote_copy(
            src_ref=moves[i][0], dst_ref=moves[i][1],
            send_sem=halo_send.at[i], recv_sem=halo_recv.at[i],
            device_id=at(mr + way[0], mc + way[1]), device_id_type=MESH,
        )

    def regroup(x, y, z, kinds):
        quarter = iota(x.shape, 1) // HEAD_DIM
        def choose(a, b, c, e):
            return jnp.where(quarter < 2, jnp.where(quarter == 0, a, b), jnp.where(quarter == 2, c, e))

        def turn(a, n):
            return pltpu.roll(a, n * HEAD_DIM, 1)

        makers = (
            lambda: choose(x, turn(x, 2), y, turn(z, 2)),
            lambda: choose(turn(x, 3), turn(y, 1), turn(y, 3), turn(z, 1)),
            lambda: choose(turn(x, 2), y, turn(z, 2), z),
        )
        return [(t, makers[t]()) for t in kinds]

    def order_weights(kinds):
        for i in range(n_chunk):
            native = [w_ref[:, (3 * i + t) * LANES : (3 * i + t + 1) * LANES] for t in range(3)]
            for t, tile in regroup(*native, kinds):
                wq[:, t * d + i * LANES : t * d + (i + 1) * LANES] = tile

    def put(ch, row, block):
        stag[ch, pl.ds(row * pitch + PAD, breadth), :] = block

    tokens = tok_ref[...].reshape(amount, d)

    def project(first, last):
        for p in range(first, last):
            y = dot(tokens, wq[:, p * PACK : (p + 1) * PACK])
            for c in range(PACK // LANES):
                for r in range(height):
                    put(2 * p + c, r + 2, y[r * breadth : (r + 1) * breadth, c * LANES : (c + 1) * LANES])

    fetch(1).wait()
    order_weights((1, 2))
    project(n_pack, 3 * n_pack)

    if paired:
        pl.semaphore_wait(barrier, n_all - 1)
    else:
        n_diag = sum(exists(way).astype(jnp.int32) for way in WAYS[4:])
        pl.semaphore_wait(barrier, n_rows - 1 + n_cols - 1 + n_diag)
    for i, way in enumerate(WAYS):
        @pl.when(exists(way))
        def _():
            halo_copy(i).start()

        @pl.when(jnp.logical_not(exists((-way[0], -way[1]))))
        def _():
            dst = moves[i][1]
            dst[...] = jnp.zeros(dst.shape, BF)


    prow, pcol = iota((PACK, PACK), 0), iota((PACK, PACK), 1)
    same = prow // HEAD_DIM == pcol // HEAD_DIM
    same_hot = one_hot(same)
    dn = (((0,), (0,)), ((), ()))

    def local_states(z, get_k, get_v):
        blank_rows = jnp.zeros((SUB - 1, PACK), F32)
        pieces = []
        for i in range(n_pack):
            k = feature_map(get_k(i))
            st = lax.dot_general(k.astype(BF), get_v(i).astype(BF), dn, preferred_element_type=F32)
            st = jnp.sum(jnp.where(same, st, 0.0).reshape(8, HEAD_DIM, PACK), axis=0)
            pieces.append(jnp.concatenate([st, jnp.sum(k, axis=0, keepdims=True), blank_rows], axis=0))
        if paired:
            for i in range(n_pack):
                part[z, i] = pieces[i]
        else:
            flat = jnp.concatenate(pieces, axis=1)
            step = ROWS // n_cols
            for q in range(n_cols):
                part[z, q] = flat[q * step : (q + 1) * step]

    side = lax.rem(mc, 2)
    half_cols = max(n_cols // 2, 1)
    n_chips = n_rows * half_cols if paired else 0
    slot = side if paired else mc
    ways = 2 if paired else n_cols

    def rs_copy(z, k):
        peer = mc + 1 - 2 * side if paired else lax.rem(mc + k, n_cols)
        return pltpu.make_async_remote_copy(
            src_ref=part.at[z, 1 - side if paired else peer], dst_ref=rs.at[z, k - 1],
            send_sem=red_send.at[z, 0, k - 1], recv_sem=red_recv.at[z, 0, k - 1],
            device_id=at(mr, peer), device_id_type=MESH,
        )

    n_far = n_chips if paired else n_rows

    def ar_copy(z, k):
        if paired:
            chip = lax.rem(mr * half_cols + mc // 2 + k, n_chips)
            device = at(chip // half_cols, 2 * lax.rem(chip, half_cols) + side)
        else:
            device = at(lax.rem(mr + k, n_rows), mc)
        return pltpu.make_async_remote_copy(
            src_ref=ar_src.at[z], dst_ref=ar.at[z, k - 1],
            send_sem=red_send.at[z, 1, k - 1], recv_sem=red_recv.at[z, 1, k - 1],
            device_id=device, device_id_type=MESH,
        )

    def ag_copy(z, k, back=False):
        if paired:
            peer, other = mc + 1 - 2 * side, 1 - side
        else:
            peer = other = lax.rem(mc + (n_cols - k if back else k), n_cols)
        return pltpu.make_async_remote_copy(
            src_ref=ag.at[z, slot], dst_ref=ag.at[z, other if back else slot],
            send_sem=red_send.at[z, 2, k - 1], recv_sem=red_recv.at[z, 2, k - 1],
            device_id=at(mr, peer), device_id_type=MESH,
        )

    def reduce_1(z):
        for k in range(1, ways):
            rs_copy(z, k).start()

    def reduce_2(z):
        total = part[z, slot]
        for k in range(1, ways):
            rs_copy(z, k).wait_recv()
            total = total + rs[z, k - 1]
        ar_src[z] = total.astype(ar_src.dtype)
        for k in range(1, n_far):
            ar_copy(z, k).start()

    def reduce_3(z):
        total = ar_src[z].astype(F32)
        for k in range(1, n_far):
            ar_copy(z, k).wait_recv()
            total = total + ar[z, k - 1].astype(F32)
        ag[z, slot] = total
        for k in range(1, ways):
            ag_copy(z, k).start()

    def reduce_4(z):
        for k in range(1, ways):
            ag_copy(z, k, back=True).wait_recv()
        return jnp.concatenate([ag[z, q] for q in range(ways)], axis=1 if paired else 0)

    def conv(first, last, start_row, n_lines, hop, count):
        def chunk(ch, _):
            w = [jnp.broadcast_to(taps[ch, t : t + 1, :], (SUB, LANES)).astype(BF) for t in range(25)]

            def lines(q, _):
                r0 = start_row + q * hop
                sums = [[None] * inner for _ in range(n_lines)]
                for rr in range(n_lines + 4):
                    start = (r0 + rr) * pitch + PAD - 2
                    xs = [stag[ch, pl.ds(start + jj, SUB, stride=inner), :].astype(BF) for jj in range(wide)]
                    for n in range(n_lines):
                        a = rr - n
                        if 0 <= a < 5:
                            for j in range(inner):
                                term = xs[j] * w[5 * a]
                                for b in range(1, 5):
                                    term = term + xs[j + b] * w[5 * a + b]
                                sums[n][j] = term if a == 0 else sums[n][j] + term
                for n in range(n_lines):
                    for j in range(inner):
                        spread[ch, pl.ds((r0 + n) * breadth + j, SUB, stride=inner), :] = sums[n][j].astype(F32)
                return 0

            lax.fori_loop(0, count, lines, 0)
            return 0

        lax.fori_loop(first, last, chunk, 0)

    def native(t, i):
        lo = (t * d + i * PACK) // LANES
        return jnp.concatenate(
            [
                jnp.concatenate([stag[lo + c, pl.ds((r + 2) * pitch + PAD, breadth), :] for r in range(height)], axis=0)
                for c in range(PACK // LANES)
            ],
            axis=1,
        )

    def grouped(t, i):
        lo = (t * d + i * PACK) // LANES
        x = jnp.concatenate([spread[lo + c].astype(BF) for c in range(PACK // LANES)], axis=1)
        return dot(x, gbd[t * n_pack + i])

    def mix_states(z, flat):
        for i in range(n_pack):
            rows = slice(z * d + i * PACK, z * d + (i + 1) * PACK)
            st = flat[:HEAD_DIM, i * PACK : (i + 1) * PACK]
            st = jnp.where(same, jnp.concatenate([st] * 8, axis=0), 0.0).astype(BF)
            mix[i * PACK : (i + 1) * PACK, :] = (dot(st, pw_ref[rows, :]) * gain_ref[...]).astype(BF)

    def attend(flat, get_q):
        heads = []
        for i in range(n_pack):
            tot = flat[HEAD_DIM : HEAD_DIM + 1, i * PACK : (i + 1) * PACK]
            q = get_q(i)
            den = dot((q * tot).astype(BF), same_hot)
            heads.append((q * pl.reciprocal(den, approx=True)).astype(BF))
        return dot(jnp.concatenate(heads, axis=1), mix[...])

    local_states(0, lambda i: native(1, i), lambda i: native(2, i))
    reduce_1(0)
    fetch(2).wait()
    for i in range(n_chunk):
        native_taps = [dk_ref[:, (3 * i + t) * LANES : (3 * i + t + 1) * LANES] for t in range(3)]
        for t, tile in regroup(*native_taps, (0, 1, 2)):
            taps[t * n_chunk + i, :25, :] = tile

    fetch(3).wait()
    n_group = gk_ref.shape[2]
    eye = one_hot(iota((n_group, n_group), 0) == iota((n_group, n_group), 1))
    flat_gk = gk_ref[...].reshape(HEAD_DIM * HEAD_DIM, n_group)
    turned = lax.dot_general(eye, flat_gk, (((1,), (1,)), ((), ())), preferred_element_type=F32)
    quarter = iota((n_group, LANES), 1) // HEAD_DIM
    for k in range(HEAD_DIM * HEAD_DIM // LANES):
        tile = turned[:, k * LANES : (k + 1) * LANES]
        turns = [tile] + [pltpu.roll(tile, n * HEAD_DIM, 1) for n in range(1, 4)]
        for j in range(4):
            t0, t1, t2, t3 = (turns[(b - j) % 4] for b in range(4))
            copy = jnp.where(quarter < 2, jnp.where(quarter == 0, t0, t1), jnp.where(quarter == 2, t2, t3))
            gsq[pl.ds(4 * k + j, n_group, stride=HEAD_DIM), :] = copy
    own = iota((LANES, LANES), 0) // HEAD_DIM == iota((LANES, LANES), 1) // HEAD_DIM
    blank = jnp.zeros((LANES, LANES), BF)
    for t in range(3):
        for i in range(n_pack):
            blocks = []
            for c in range(PACK // LANES):
                base = 4 * (2 * i + c)
                block = jnp.concatenate(
                    [gsq[(3 * (base + h) + t) * HEAD_DIM : (3 * (base + h) + t + 1) * HEAD_DIM, :] for h in range(4)], axis=0)
                blocks.append(jnp.where(own, block, 0.0).astype(BF))
            gbd[t * n_pack + i, :LANES, :] = jnp.concatenate([blocks[0], blank], axis=1)
            gbd[t * n_pack + i, LANES:, :] = jnp.concatenate([blank, blocks[1]], axis=1)

    def arrived(which):
        for i in which:
            way = WAYS[i]

            @pl.when(exists((-way[0], -way[1])))
            def _():
                halo_copy(i).wait_recv()

    def project_sides(first, last):
        around = halo_e[...].reshape(2 * e, d)
        for p in range(first, last):
            y = dot(around, wq[:, p * PACK : (p + 1) * PACK])
            for c in range(PACK // LANES):
                for side in range(2):
                    for b in range(2):
                        col = (breadth + PAD if side else PAD - 2) + b
                        lo = side * e + b * height
                        stag[2 * p + c, pl.ds(2 * pitch + col, height, stride=pitch), :] = (
                            y[lo : lo + height, c * LANES : (c + 1) * LANES])

    def project_rows(first, last):
        around = jnp.concatenate([halo_r[...].reshape(4 * breadth, d), halo_c[...].reshape(4 * SUB, d)], axis=0)
        for p in range(first, last):
            y = dot(around, wq[:, p * PACK : (p + 1) * PACK])
            for c in range(PACK // LANES):
                ch = 2 * p + c
                cut = y[:, c * LANES : (c + 1) * LANES]
                for n, row in enumerate((0, 1, height + 2, height + 3)):
                    put(ch, row, cut[n * breadth : (n + 1) * breadth])
                for side in range(2):
                    for b in range(2):
                        col = (breadth + PAD if side else PAD - 2) + b
                        for n in range(2):
                            lo = 4 * breadth + (2 * n + side) * SUB + 2 * b
                            row = n * (height + 2)
                            stag[ch, pl.ds(row * pitch + col, 2, stride=pitch), :] = cut[lo : lo + 2]

    arrived((2, 3))
    project_sides(n_pack, 3 * n_pack)
    reduce_2(0)
    conv(n_chunk, 3 * n_chunk, 2, LINES, LINES, (height - 4) // LINES)
    arrived((0, 1, 4, 5, 6, 7))
    project_rows(n_pack, 3 * n_pack)
    conv(n_chunk, 3 * n_chunk, 0, 2, height - 2, 2)
    local_states(1, lambda i: grouped(1, i), lambda i: grouped(2, i))
    reduce_1(1)
    reduce_3(0)
    order_weights((0,))
    project(0, n_pack)
    reduce_2(1)
    project_sides(0, n_pack)
    project_rows(0, n_pack)
    whole = (0, LINES, LINES, height // LINES)
    conv(0, n_chunk, *whole)
    for i in range(4, 7):
        fetch(i).wait()
    flat = reduce_4(0)
    mix_states(0, flat)
    acc[...] = attend(flat, lambda i: feature_map(native(0, i))) + (tokens.astype(F32) + bias_ref[...])
    reduce_3(1)
    for i in range(n_pack):
        q = feature_map(grouped(0, i))
        for c in range(PACK // LANES):
            spread[2 * i + c] = q[:, c * LANES : (c + 1) * LANES]
    flat = reduce_4(1)
    mix_states(1, flat)
    n_part = 2
    piece = height // n_part

    def store(b):
        rows = pl.ds(b * piece, piece)
        return pltpu.make_async_copy(result.at[rows], out_ref.at[rows], done.at[b])

    for b in range(n_part):
        cut = slice(b * piece * breadth, (b + 1) * piece * breadth)
        late = [
            jnp.concatenate([spread[2 * i + c, cut] for c in range(PACK // LANES)], axis=1) for i in range(n_pack)
        ]
        got = acc[cut] + attend(flat, lambda i: late[i])
        result[b * piece : (b + 1) * piece] = got.astype(BF).reshape(piece, breadth, d)
        store(b).start()
    for b in range(n_part):
        store(b).wait()

    for i, way in enumerate(WAYS):
        @pl.when(exists(way))
        def _():
            halo_copy(i).wait_send()
    for z in range(2):
        for k in range(1, ways):
            rs_copy(z, k).wait_send()
            ag_copy(z, k).wait_send()
        for k in range(1, n_far):
            ar_copy(z, k).wait_send()


def finish(src, out, sem):
    copy = pltpu.make_async_copy(src, out, sem)
    copy.start()
    copy.wait()


def body(n_rows, n_cols, tokens, qkv_weight, depth_kernel, group_kernel, proj_weight, out_gain, out_bias):
    height, breadth, d = tokens.shape
    paired = is_paired(n_rows, n_cols, d)
    ways, far = (2, n_rows * n_cols // 2) if paired else (n_cols, n_rows)
    block = (ROWS, PACK) if paired else (ROWS // n_cols, d)
    far_type = BF if paired else F32
    most = max(far, ways)
    operands = (
        tokens, qkv_weight, depth_kernel, jnp.transpose(group_kernel, (1, 2, 0)), proj_weight, out_gain[None, :], out_bias[None, :])
    operands = [pltpu.with_memory_space_constraint(x, pltpu.HBM) for x in operands]
    mixed = pl.pallas_call(
        functools.partial(kernel, n_rows, n_cols),
        out_shape=jax.ShapeDtypeStruct((height, breadth, d), BF),
        in_specs=[pl.BlockSpec(memory_space=pl.ANY)] * 7,
        out_specs=pl.BlockSpec(memory_space=pl.ANY),
        scratch_shapes=[pltpu.VMEM(x.shape, x.dtype) for x in operands] + [
            pltpu.VMEM((2, 2 * height, d), BF),
            pltpu.VMEM((4, SUB, d), BF),
            pltpu.VMEM((2, 2 * height, d), BF),
            pltpu.VMEM((4, SUB, d), BF),
            pltpu.VMEM((2, 2, breadth, d), BF),
            pltpu.VMEM((d, 3 * d), BF),
            pltpu.VMEM((3 * d // LANES, 32, LANES), F32),
            pltpu.VMEM((3 * d, LANES), F32),
            pltpu.VMEM((3 * d // PACK, PACK, PACK), BF),
            pltpu.VMEM((3 * d // LANES, (height + 4) * (breadth + 2 * PAD), LANES), F32),
            pltpu.VMEM((3 * d // LANES, height * breadth, LANES), F32),
            pltpu.VMEM((height * breadth, d), F32),
            pltpu.VMEM((d, d), BF),
            pltpu.VMEM((height, breadth, d), BF),
            pltpu.VMEM((2, ways, *block), F32),
            pltpu.VMEM((2, ways - 1, *block), F32),
            pltpu.VMEM((2, *block), far_type),
            pltpu.VMEM((2, far - 1, *block), far_type),
            pltpu.VMEM((2, ways, *block), F32),
            pltpu.SemaphoreType.DMA((8,)),
            pltpu.SemaphoreType.DMA((8,)),
            pltpu.SemaphoreType.DMA((2, 3, most)),
            pltpu.SemaphoreType.DMA((2, 3, most)),
            pltpu.SemaphoreType.DMA((7,)),
            pltpu.SemaphoreType.DMA((2,)),
        ],
        compiler_params=pltpu.CompilerParams(
            collective_id=0, has_side_effects=True, vmem_limit_bytes=48 * 1024 * 1024
        ),
        name="attention_module",
    )(*operands)
    return pl.pallas_call(
        finish,
        out_shape=jax.ShapeDtypeStruct((height, breadth, d), BF),
        in_specs=[pl.BlockSpec(memory_space=pl.ANY)],
        out_specs=pl.BlockSpec(memory_space=pl.ANY),
        scratch_shapes=[pltpu.SemaphoreType.DMA],
        compiler_params=pltpu.CompilerParams(vmem_limit_bytes=4 * 1024 * 1024),
        name="finish",
    )(mixed)


def solution(mesh):
    placed = (P(("groups", "rows"), "cols", None), P(), P(), P(), P(), P(), P())
    return jax.shard_map(
        functools.partial(body, mesh.shape["rows"], mesh.shape["cols"]),
        mesh=mesh,
        in_specs=placed,
        out_specs=P(("groups", "rows"), "cols", None),
        check_vma=False,
    )
```

```python
import functools

import jax
import jax.numpy as jnp
from jax import lax
from jax.experimental import pallas as pl
from jax.experimental.pallas import tpu as pltpu
from jax.sharding import PartitionSpec as P

HEAD_DIM = 32
PACK = 8 * HEAD_DIM
LANES = 128
SUB = 16
PAD = 8
LINES = 4
ROWS = HEAD_DIM + 8
BF = jnp.bfloat16
F32 = jnp.float32
WAYS = ((1, 0), (-1, 0), (0, 1), (0, -1), (1, 1), (1, -1), (-1, 1), (-1, -1))


def is_paired(n_rows, n_cols, d):
    return n_cols % 2 == 0 and n_rows * n_cols <= 32 and d == 2 * PACK


def iota(shape, dim):
    return lax.broadcasted_iota(jnp.int32, shape, dim)


def dot(a, b):
    return jnp.dot(a, b, preferred_element_type=F32)


def feature_map(u):
    return jnp.where(u > 0, u + 1.0, jnp.exp(jnp.minimum(u, 0.0)))


def one_hot(mask):
    return jnp.where(mask, 1.0, 0.0).astype(BF)


def kernel(
    n_rows, n_cols,
    *refs,
):
    sources, out_ref, refs = refs[:7], refs[7], refs[8:]
    inputs, refs = refs[:7], refs[7:]
    tok_ref, w_ref, dk_ref, gk_ref, pw_ref, gain_ref, bias_ref = inputs
    (
    stage_e, stage_c, halo_e, halo_c, halo_r, wq, taps, gsq, gbd, stag, spread, acc, mix,
    part, rs, ar_src, ar, tot_src, tots, ag,
    halo_send, halo_recv, red_send, red_recv, load,
    ) = refs

    def fetch(i):
        return pltpu.make_async_copy(sources[i], inputs[i], load.at[i])

    for i in range(7):
        fetch(i).start()
    height, breadth, d = tok_ref.shape
    inner = breadth // SUB
    wide = inner + 4
    amount = height * breadth
    n_pack = d // PACK
    n_chunk = d // LANES
    pitch = breadth + 2 * PAD
    mr, mc = lax.axis_index("rows"), lax.axis_index("cols")

    def exists(way):
        r, c = mr + way[0], mc + way[1]
        return (r >= 0) & (r < n_rows) & (c >= 0) & (c < n_cols)

    def at(r, c):
        return {"rows": r, "cols": c}

    MESH = pl.DeviceIdType.MESH
    barrier = pltpu.get_barrier_semaphore()
    n_all = n_rows * n_cols
    paired = is_paired(n_rows, n_cols, d)
    me = mr * n_cols + mc
    if paired:
        for k in range(1, n_all):
            peer = lax.rem(me + k, n_all)
            pl.semaphore_signal(
                barrier, inc=1, device_id=at(peer // n_cols, lax.rem(peer, n_cols)), device_id_type=MESH)
    else:
        for k in range(1, n_rows):
            pl.semaphore_signal(barrier, inc=1, device_id=at(lax.rem(mr + k, n_rows), mc), device_id_type=MESH)
        for k in range(1, n_cols):
            pl.semaphore_signal(barrier, inc=1, device_id=at(mr, lax.rem(mc + k, n_cols)), device_id_type=MESH)
        for way in WAYS[4:]:
            @pl.when(exists(way))
            def _():
                pl.semaphore_signal(barrier, inc=1, device_id=at(mr + way[0], mc + way[1]), device_id_type=MESH)

    fetch(0).wait()
    e = 2 * height
    rows_out = 2 * e + 4 * SUB
    m = iota((rows_out, amount), 0)
    src = iota((rows_out, amount), 1)
    right = (m >= e).astype(jnp.int32)
    me_ = m - right * e
    edge = (me_ % height) * breadth + me_ // height + right * (breadth - 2)
    cm = m - 2 * e
    ci, cr = cm // SUB, cm % SUB
    corner = ((cr % 2) + (ci // 2) * (height - 2)) * breadth + (cr // 2) + (ci % 2) * (breadth - 2)
    want = jnp.where(m < 2 * e, edge, jnp.where(cr < 4, corner, -1))
    sel = dot(one_hot(want == src), tok_ref[...].reshape(amount, d)).astype(BF)
    stage_e[...] = sel[: 2 * e].reshape(2, e, d)
    stage_c[...] = sel[2 * e :].reshape(4, SUB, d)

    moves = (
        (tok_ref.at[pl.ds(height - 2, 2)], halo_r.at[0]),
        (tok_ref.at[pl.ds(0, 2)], halo_r.at[1]),
        (stage_e.at[1], halo_e.at[0]),
        (stage_e.at[0], halo_e.at[1]),
        (stage_c.at[3], halo_c.at[0]),
        (stage_c.at[2], halo_c.at[1]),
        (stage_c.at[1], halo_c.at[2]),
        (stage_c.at[0], halo_c.at[3]),
    )

    def halo_copy(i):
        way = WAYS[i]
        return pltpu.make_async_remote_copy(
            src_ref=moves[i][0], dst_ref=moves[i][1],
            send_sem=halo_send.at[i], recv_sem=halo_recv.at[i],
            device_id=at(mr + way[0], mc + way[1]), device_id_type=MESH,
        )

    def regroup(x, y, z, kinds):
        quarter = iota(x.shape, 1) // HEAD_DIM
        def choose(a, b, c, e):
            return jnp.where(quarter < 2, jnp.where(quarter == 0, a, b), jnp.where(quarter == 2, c, e))

        def turn(a, n):
            return pltpu.roll(a, n * HEAD_DIM, 1)

        makers = (
            lambda: choose(x, turn(x, 2), y, turn(z, 2)),
            lambda: choose(turn(x, 3), turn(y, 1), turn(y, 3), turn(z, 1)),
            lambda: choose(turn(x, 2), y, turn(z, 2), z),
        )
        return [(t, makers[t]()) for t in kinds]

    def order_weights(kinds):
        for i in range(n_chunk):
            native = [w_ref[:, (3 * i + t) * LANES : (3 * i + t + 1) * LANES] for t in range(3)]
            for t, tile in regroup(*native, kinds):
                wq[:, t * d + i * LANES : t * d + (i + 1) * LANES] = tile

    def put(ch, row, block):
        stag[ch, pl.ds(row * pitch + PAD, breadth), :] = block

    tokens = tok_ref[...].reshape(amount, d)

    def project(first, last):
        for p in range(first, last):
            y = dot(tokens, wq[:, p * PACK : (p + 1) * PACK])
            for c in range(PACK // LANES):
                for r in range(height):
                    put(2 * p + c, r + 2, y[r * breadth : (r + 1) * breadth, c * LANES : (c + 1) * LANES])

    fetch(1).wait()
    order_weights((1, 2))
    project(n_pack, 3 * n_pack)

    if paired:
        pl.semaphore_wait(barrier, n_all - 1)
    else:
        n_diag = sum(exists(way).astype(jnp.int32) for way in WAYS[4:])
        pl.semaphore_wait(barrier, n_rows - 1 + n_cols - 1 + n_diag)
    for i, way in enumerate(WAYS):
        @pl.when(exists(way))
        def _():
            halo_copy(i).start()

        @pl.when(jnp.logical_not(exists((-way[0], -way[1]))))
        def _():
            dst = moves[i][1]
            dst[...] = jnp.zeros(dst.shape, BF)


    prow, pcol = iota((PACK, PACK), 0), iota((PACK, PACK), 1)
    same = prow // HEAD_DIM == pcol // HEAD_DIM
    same_hot = one_hot(same)
    dn = (((0,), (0,)), ((), ()))

    def local_states(z, get_k, get_v):
        blank_rows = jnp.zeros((ROWS - HEAD_DIM - 1, PACK), F32)
        pieces = []
        for i in range(n_pack):
            k = feature_map(get_k(i))
            st = lax.dot_general(k.astype(BF), get_v(i).astype(BF), dn, preferred_element_type=F32)
            st = jnp.sum(jnp.where(same, st, 0.0).reshape(8, HEAD_DIM, PACK), axis=0)
            pieces.append(jnp.concatenate([st, jnp.sum(k, axis=0, keepdims=True), blank_rows], axis=0))
        if paired:
            for i in range(n_pack):
                part[z, i] = pieces[i]
        else:
            flat = jnp.concatenate(pieces, axis=1)
            step = ROWS // n_cols
            for q in range(n_cols):
                part[z, q] = flat[q * step : (q + 1) * step]

    side = lax.rem(mc, 2)
    half_cols = max(n_cols // 2, 1)
    n_chips = n_rows * half_cols if paired else 0
    slot = side if paired else mc
    ways = 2 if paired else n_cols

    def rs_copy(z, k):
        peer = mc + 1 - 2 * side if paired else lax.rem(mc + k, n_cols)
        return pltpu.make_async_remote_copy(
            src_ref=part.at[z, 1 - side if paired else peer], dst_ref=rs.at[z, k - 1],
            send_sem=red_send.at[z, 0, k - 1], recv_sem=red_recv.at[z, 0, k - 1],
            device_id=at(mr, peer), device_id_type=MESH,
        )

    n_far = n_chips if paired else n_rows

    def far_device(k):
        if paired:
            chip = lax.rem(mr * half_cols + mc // 2 + k, n_chips)
            device = at(chip // half_cols, 2 * lax.rem(chip, half_cols) + side)
        else:
            device = at(lax.rem(mr + k, n_rows), mc)
        return device

    def ar_copy(z, k):
        return pltpu.make_async_remote_copy(
            src_ref=ar_src.at[z], dst_ref=ar.at[z, k - 1],
            send_sem=red_send.at[z, 1, k - 1], recv_sem=red_recv.at[z, 1, k - 1],
            device_id=far_device(k), device_id_type=MESH,
        )

    def tot_copy(z, k):
        return pltpu.make_async_remote_copy(
            src_ref=tot_src.at[z], dst_ref=tots.at[z, k - 1],
            send_sem=red_send.at[z, 3, k - 1], recv_sem=red_recv.at[z, 3, k - 1],
            device_id=far_device(k), device_id_type=MESH,
        )

    def ag_copy(z, k, back=False):
        if paired:
            peer, other = mc + 1 - 2 * side, 1 - side
        else:
            peer = other = lax.rem(mc + (n_cols - k if back else k), n_cols)
        return pltpu.make_async_remote_copy(
            src_ref=ag.at[z, slot], dst_ref=ag.at[z, other if back else slot],
            send_sem=red_send.at[z, 2, k - 1], recv_sem=red_recv.at[z, 2, k - 1],
            device_id=at(mr, peer), device_id_type=MESH,
        )

    def reduce_1(z):
        for k in range(1, ways):
            rs_copy(z, k).start()

    def reduce_2(z):
        total = part[z, slot]
        for k in range(1, ways):
            rs_copy(z, k).wait_recv()
            total = total + rs[z, k - 1]
        if paired:
            ar_src[z] = total[:HEAD_DIM].astype(BF)
            tot_src[z] = total[HEAD_DIM : HEAD_DIM + 1]
        else:
            ar_src[z] = total
        for k in range(1, n_far):
            ar_copy(z, k).start()
            if paired:
                tot_copy(z, k).start()

    def reduce_3(z):
        total = ar_src[z].astype(F32)
        tot = tot_src[z]
        for k in range(1, n_far):
            ar_copy(z, k).wait_recv()
            total = total + ar[z, k - 1].astype(F32)
            if paired:
                tot_copy(z, k).wait_recv()
                tot = tot + tots[z, k - 1]
        if paired:
            total = jnp.concatenate([total, tot, jnp.zeros((ROWS - HEAD_DIM - 1, PACK), F32)], axis=0)
        ag[z, slot] = total
        for k in range(1, ways):
            ag_copy(z, k).start()

    def reduce_4(z):
        for k in range(1, ways):
            ag_copy(z, k, back=True).wait_recv()
        return jnp.concatenate([ag[z, q] for q in range(ways)], axis=1 if paired else 0)

    def conv(first, last, start_row, n_lines, hop, count):
        def chunk(ch, _):
            w = [jnp.broadcast_to(taps[ch, t : t + 1, :], (SUB, LANES)).astype(BF) for t in range(25)]

            def lines(q, _):
                r0 = start_row + q * hop
                sums = [[None] * inner for _ in range(n_lines)]
                for rr in range(n_lines + 4):
                    start = (r0 + rr) * pitch + PAD - 2
                    xs = [stag[ch, pl.ds(start + jj, SUB, stride=inner), :].astype(BF) for jj in range(wide)]
                    for n in range(n_lines):
                        a = rr - n
                        if 0 <= a < 5:
                            for j in range(inner):
                                term = xs[j] * w[5 * a]
                                for b in range(1, 5):
                                    term = term + xs[j + b] * w[5 * a + b]
                                sums[n][j] = term if a == 0 else sums[n][j] + term
                for n in range(n_lines):
                    for j in range(inner):
                        spread[ch, pl.ds((r0 + n) * breadth + j, SUB, stride=inner), :] = sums[n][j].astype(F32)
                return 0

            lax.fori_loop(0, count, lines, 0)
            return 0

        lax.fori_loop(first, last, chunk, 0)

    def native(t, i):
        lo = (t * d + i * PACK) // LANES
        return jnp.concatenate(
            [
                jnp.concatenate([stag[lo + c, pl.ds((r + 2) * pitch + PAD, breadth), :] for r in range(height)], axis=0)
                for c in range(PACK // LANES)
            ],
            axis=1,
        )

    def grouped(t, i):
        lo = (t * d + i * PACK) // LANES
        x = jnp.concatenate([spread[lo + c].astype(BF) for c in range(PACK // LANES)], axis=1)
        return dot(x, gbd[t * n_pack + i])

    def mix_states(z, flat):
        for i in range(n_pack):
            rows = slice(z * d + i * PACK, z * d + (i + 1) * PACK)
            st = flat[:HEAD_DIM, i * PACK : (i + 1) * PACK]
            st = jnp.where(same, jnp.concatenate([st] * 8, axis=0), 0.0).astype(BF)
            mix[i * PACK : (i + 1) * PACK, :] = (dot(st, pw_ref[rows, :]) * gain_ref[...]).astype(BF)

    def attend(flat, get_q):
        heads = []
        for i in range(n_pack):
            tot = flat[HEAD_DIM : HEAD_DIM + 1, i * PACK : (i + 1) * PACK]
            q = get_q(i)
            den = dot((q * tot).astype(BF), same_hot)
            heads.append((q * pl.reciprocal(den, approx=True)).astype(BF))
        return dot(jnp.concatenate(heads, axis=1), mix[...])

    local_states(0, lambda i: native(1, i), lambda i: native(2, i))
    reduce_1(0)
    def order_taps(kinds):
        for i in range(n_chunk):
            native_taps = [dk_ref[:, (3 * i + t) * LANES : (3 * i + t + 1) * LANES] for t in range(3)]
            for t, tile in regroup(*native_taps, kinds):
                taps[t * n_chunk + i, :25, :] = tile

    n_group = gk_ref.shape[2]
    heads_each = n_group // 3
    quarter = iota((heads_each, LANES), 1) // HEAD_DIM
    own = iota((LANES, LANES), 0) // HEAD_DIM == iota((LANES, LANES), 1) // HEAD_DIM
    blank = jnp.zeros((LANES, LANES), BF)

    def order_groups(kinds):
        flat_gk = gk_ref[...].reshape(HEAD_DIM * HEAD_DIM, n_group)
        for t in kinds:
            pick = one_hot(3 * iota((heads_each, n_group), 0) + t == iota((heads_each, n_group), 1))
            turned = lax.dot_general(pick, flat_gk, (((1,), (1,)), ((), ())), preferred_element_type=F32)
            for k in range(HEAD_DIM * HEAD_DIM // LANES):
                tile = turned[:, k * LANES : (k + 1) * LANES]
                turns = [tile] + [pltpu.roll(tile, n * HEAD_DIM, 1) for n in range(1, 4)]
                for j in range(4):
                    t0, t1, t2, t3 = (turns[(b - j) % 4] for b in range(4))
                    copy = jnp.where(quarter < 2, jnp.where(quarter == 0, t0, t1), jnp.where(quarter == 2, t2, t3))
                    gsq[pl.ds(t * d + 4 * k + j, heads_each, stride=HEAD_DIM), :] = copy
            for i in range(n_pack):
                blocks = []
                for c in range(PACK // LANES):
                    block = gsq[t * d + (2 * i + c) * LANES : t * d + (2 * i + c + 1) * LANES, :]
                    blocks.append(jnp.where(own, block, 0.0).astype(BF))
                gbd[t * n_pack + i, :LANES, :] = jnp.concatenate([blocks[0], blank], axis=1)
                gbd[t * n_pack + i, LANES:, :] = jnp.concatenate([blank, blocks[1]], axis=1)

    def arrived(which):
        for i in which:
            way = WAYS[i]

            @pl.when(exists((-way[0], -way[1])))
            def _():
                halo_copy(i).wait_recv()

    def project_sides(first, last, repair=False):
        around = halo_e[...].reshape(2 * e, d)
        for p in range(first, last):
            y = dot(around, wq[:, p * PACK : (p + 1) * PACK])
            for c in range(PACK // LANES):
                for side in range(2):
                    for b in range(2):
                        col = (breadth + PAD if side else PAD - 2) + b
                        lo = side * e + b * height
                        stag[2 * p + c, pl.ds(2 * pitch + col, height, stride=pitch), :] = (
                            y[lo : lo + height, c * LANES : (c + 1) * LANES])
                if repair:
                    repair_rows(2 * p + c, y[:, c * LANES : (c + 1) * LANES])

    def repair_rows(ch, y):
        n = height - 4

        def part_sum(side, terms):
            total = None
            for b, tap in terms:
                for a in range(5):
                    lo = side * e + b * height + a
                    term = y[lo : lo + n] * taps[ch, 5 * a + tap : 5 * a + tap + 1, :]
                    total = term if total is None else total + term
            return total

        for col, side, terms in (
            (0, 0, ((0, 0), (1, 1))),
            (1, 0, ((1, 0),)),
            (breadth - 2, 1, ((0, 4),)),
            (breadth - 1, 1, ((0, 3), (1, 4))),
        ):
            rows = pl.ds(2 * breadth + col, n, stride=breadth)
            spread[ch, rows, :] = spread[ch, rows, :] + part_sum(side, terms)

    def project_rows(first, last):
        around = jnp.concatenate([halo_r[...].reshape(4 * breadth, d), halo_c[...].reshape(4 * SUB, d)], axis=0)
        for p in range(first, last):
            y = dot(around, wq[:, p * PACK : (p + 1) * PACK])
            for c in range(PACK // LANES):
                ch = 2 * p + c
                cut = y[:, c * LANES : (c + 1) * LANES]
                for n, row in enumerate((0, 1, height + 2, height + 3)):
                    put(ch, row, cut[n * breadth : (n + 1) * breadth])
                for side in range(2):
                    for b in range(2):
                        col = (breadth + PAD if side else PAD - 2) + b
                        for n in range(2):
                            lo = 4 * breadth + (2 * n + side) * SUB + 2 * b
                            row = n * (height + 2)
                            stag[ch, pl.ds(row * pitch + col, 2, stride=pitch), :] = cut[lo : lo + 2]

    fetch(2).wait()
    order_taps((1, 2))
    fetch(3).wait()
    order_groups((1, 2))
    reduce_2(0)
    gap = jnp.zeros((PAD, LANES), F32)
    for ch in range(n_chunk, 3 * n_chunk):
        for r in range(2, height + 2):
            stag[ch, r * pitch : r * pitch + PAD, :] = gap
            stag[ch, r * pitch + PAD + breadth : (r + 1) * pitch, :] = gap
    conv(n_chunk, 3 * n_chunk, 2, LINES, LINES, (height - 4) // LINES)
    arrived((2, 3))
    project_sides(n_pack, 3 * n_pack, repair=True)
    arrived((0, 1, 4, 5, 6, 7))
    project_rows(n_pack, 3 * n_pack)
    conv(n_chunk, 3 * n_chunk, 0, 2, height - 2, 2)
    local_states(1, lambda i: grouped(1, i), lambda i: grouped(2, i))
    reduce_1(1)
    order_weights((0,))
    project(0, n_pack)
    reduce_2(1)
    order_taps((0,))
    order_groups((0,))
    reduce_3(0)
    project_sides(0, n_pack)
    project_rows(0, n_pack)
    whole = (0, LINES, LINES, height // LINES)
    conv(0, n_chunk, *whole)
    for i in range(4, 7):
        fetch(i).wait()
    flat = reduce_4(0)
    mix_states(0, flat)
    acc[...] = attend(flat, lambda i: feature_map(native(0, i))) + (tokens.astype(F32) + bias_ref[...])
    reduce_3(1)
    for i in range(n_pack):
        q = feature_map(grouped(0, i))
        for c in range(PACK // LANES):
            spread[2 * i + c] = q[:, c * LANES : (c + 1) * LANES]
    flat = reduce_4(1)
    mix_states(1, flat)
    n_part = 2
    piece = height // n_part

    for b in range(n_part):
        cut = slice(b * piece * breadth, (b + 1) * piece * breadth)
        late = [
            jnp.concatenate([spread[2 * i + c, cut] for c in range(PACK // LANES)], axis=1) for i in range(n_pack)
        ]
        got = acc[cut] + attend(flat, lambda i: late[i])
        out_ref[b * piece : (b + 1) * piece] = got.astype(BF).reshape(piece, breadth, d)

    for i, way in enumerate(WAYS):
        @pl.when(exists(way))
        def _():
            halo_copy(i).wait_send()
    for z in range(2):
        for k in range(1, ways):
            rs_copy(z, k).wait_send()
            ag_copy(z, k).wait_send()
        for k in range(1, n_far):
            ar_copy(z, k).wait_send()
            if paired:
                tot_copy(z, k).wait_send()


def finish(src, out, sem):
    copy = pltpu.make_async_copy(src, out, sem)
    copy.start()
    copy.wait()


def body(n_rows, n_cols, tokens, qkv_weight, depth_kernel, group_kernel, proj_weight, out_gain, out_bias):
    height, breadth, d = tokens.shape
    paired = is_paired(n_rows, n_cols, d)
    ways, far = (2, n_rows * n_cols // 2) if paired else (n_cols, n_rows)
    block = (ROWS, PACK) if paired else (ROWS // n_cols, d)
    far_block, far_type = ((HEAD_DIM, PACK), BF) if paired else (block, F32)
    most = max(far, ways)
    operands = (
        tokens, qkv_weight, depth_kernel, jnp.transpose(group_kernel, (1, 2, 0)), proj_weight, out_gain[None, :], out_bias[None, :])
    operands = [pltpu.with_memory_space_constraint(x, pltpu.HBM) for x in operands]
    mixed = pl.pallas_call(
        functools.partial(kernel, n_rows, n_cols),
        out_shape=pltpu.VMEM((height, breadth, d), BF),
        in_specs=[pl.BlockSpec(memory_space=pl.ANY)] * 7,
        out_specs=pl.BlockSpec(memory_space=pltpu.VMEM),
        scratch_shapes=[pltpu.VMEM(x.shape, x.dtype) for x in operands] + [
            pltpu.VMEM((2, 2 * height, d), BF),
            pltpu.VMEM((4, SUB, d), BF),
            pltpu.VMEM((2, 2 * height, d), BF),
            pltpu.VMEM((4, SUB, d), BF),
            pltpu.VMEM((2, 2, breadth, d), BF),
            pltpu.VMEM((d, 3 * d), BF),
            pltpu.VMEM((3 * d // LANES, 32, LANES), F32),
            pltpu.VMEM((3 * d, LANES), F32),
            pltpu.VMEM((3 * d // PACK, PACK, PACK), BF),
            pltpu.VMEM((3 * d // LANES, (height + 4) * (breadth + 2 * PAD), LANES), F32),
            pltpu.VMEM((3 * d // LANES, height * breadth, LANES), F32),
            pltpu.VMEM((height * breadth, d), F32),
            pltpu.VMEM((d, d), BF),
            pltpu.VMEM((2, ways, *block), F32),
            pltpu.VMEM((2, ways - 1, *block), F32),
            pltpu.VMEM((2, *far_block), far_type),
            pltpu.VMEM((2, far - 1, *far_block), far_type),
            pltpu.VMEM((2, 1, PACK), F32),
            pltpu.VMEM((2, far - 1, 1, PACK), F32),
            pltpu.VMEM((2, ways, *block), F32),
            pltpu.SemaphoreType.DMA((8,)),
            pltpu.SemaphoreType.DMA((8,)),
            pltpu.SemaphoreType.DMA((2, 4, most)),
            pltpu.SemaphoreType.DMA((2, 4, most)),
            pltpu.SemaphoreType.DMA((7,)),
        ],
        compiler_params=pltpu.CompilerParams(
            collective_id=0, has_side_effects=True, vmem_limit_bytes=48 * 1024 * 1024
        ),
        name="attention_module",
    )(*operands)
    return pl.pallas_call(
        finish,
        out_shape=jax.ShapeDtypeStruct((height, breadth, d), BF),
        in_specs=[pl.BlockSpec(memory_space=pl.ANY)],
        out_specs=pl.BlockSpec(memory_space=pl.ANY),
        scratch_shapes=[pltpu.SemaphoreType.DMA],
        compiler_params=pltpu.CompilerParams(vmem_limit_bytes=4 * 1024 * 1024),
        name="finish",
    )(mixed)


def solution(mesh):
    placed = (P(("groups", "rows"), "cols", None), P(), P(), P(), P(), P(), P())
    return jax.shard_map(
        functools.partial(body, mesh.shape["rows"], mesh.shape["cols"]),
        mesh=mesh,
        in_specs=placed,
        out_specs=P(("groups", "rows"), "cols", None),
        check_vma=False,
    )
```

```python
import functools

import jax
import jax.numpy as jnp
from jax import lax
from jax.experimental import pallas as pl
from jax.experimental.pallas import tpu as pltpu
from jax.sharding import PartitionSpec as P

HEAD_DIM = 32
PACK = 8 * HEAD_DIM
LANES = 128
SUB = 16
PAD = 8
LINES = 4
ROWS = HEAD_DIM + 8
BF = jnp.bfloat16
F32 = jnp.float32
WAYS = ((1, 0), (-1, 0), (0, 1), (0, -1), (1, 1), (1, -1), (-1, 1), (-1, -1))


def is_paired(n_rows, n_cols, d):
    return n_cols % 2 == 0 and n_rows * n_cols <= 32 and d == 2 * PACK


def iota(shape, dim):
    return lax.broadcasted_iota(jnp.int32, shape, dim)


def dot(a, b):
    return jnp.dot(a, b, preferred_element_type=F32)


def feature_map(u):
    return jnp.where(u > 0, u + 1.0, jnp.exp(jnp.minimum(u, 0.0)))


def one_hot(mask):
    return jnp.where(mask, 1.0, 0.0).astype(BF)


def kernel(
    n_rows, n_cols,
    *refs,
):
    sources, out_ref, refs = refs[:7], refs[7], refs[8:]
    inputs, refs = refs[:7], refs[7:]
    tok_ref, w_ref, dk_ref, gk_ref, pw_ref, gain_ref, bias_ref = inputs
    (
    stage_e, stage_c, halo_e, halo_c, halo_r, wq, taps, gsq, gbd, stag, spread, acc, mix,
    part, rs, ar_src, ar, tot_src, tots, ag,
    halo_send, halo_recv, red_send, red_recv, load,
    ) = refs

    def fetch(i):
        return pltpu.make_async_copy(sources[i], inputs[i], load.at[i])

    for i in range(7):
        fetch(i).start()
    height, breadth, d = tok_ref.shape
    inner = breadth // SUB
    wide = inner + 4
    amount = height * breadth
    n_pack = d // PACK
    n_chunk = d // LANES
    pitch = breadth + 2 * PAD
    mr, mc = lax.axis_index("rows"), lax.axis_index("cols")

    def exists(way):
        r, c = mr + way[0], mc + way[1]
        return (r >= 0) & (r < n_rows) & (c >= 0) & (c < n_cols)

    def at(r, c):
        return {"rows": r, "cols": c}

    MESH = pl.DeviceIdType.MESH
    barrier = pltpu.get_barrier_semaphore()
    n_all = n_rows * n_cols
    paired = is_paired(n_rows, n_cols, d)
    me = mr * n_cols + mc
    if paired:
        for k in range(1, n_all):
            peer = lax.rem(me + k, n_all)
            pl.semaphore_signal(
                barrier, inc=1, device_id=at(peer // n_cols, lax.rem(peer, n_cols)), device_id_type=MESH)
    else:
        for k in range(1, n_rows):
            pl.semaphore_signal(barrier, inc=1, device_id=at(lax.rem(mr + k, n_rows), mc), device_id_type=MESH)
        for k in range(1, n_cols):
            pl.semaphore_signal(barrier, inc=1, device_id=at(mr, lax.rem(mc + k, n_cols)), device_id_type=MESH)
        for way in WAYS[4:]:
            @pl.when(exists(way))
            def _():
                pl.semaphore_signal(barrier, inc=1, device_id=at(mr + way[0], mc + way[1]), device_id_type=MESH)

    fetch(0).wait()
    e = 2 * height
    rows_out = 2 * e + 4 * SUB
    m = iota((rows_out, amount), 0)
    src = iota((rows_out, amount), 1)
    right = (m >= e).astype(jnp.int32)
    me_ = m - right * e
    edge = (me_ % height) * breadth + me_ // height + right * (breadth - 2)
    cm = m - 2 * e
    ci, cr = cm // SUB, cm % SUB
    corner = ((cr % 2) + (ci // 2) * (height - 2)) * breadth + (cr // 2) + (ci % 2) * (breadth - 2)
    want = jnp.where(m < 2 * e, edge, jnp.where(cr < 4, corner, -1))
    sel = dot(one_hot(want == src), tok_ref[...].reshape(amount, d)).astype(BF)
    stage_e[...] = sel[: 2 * e].reshape(2, e, d)
    stage_c[...] = sel[2 * e :].reshape(4, SUB, d)

    moves = (
        (tok_ref.at[pl.ds(height - 2, 2)], halo_r.at[0]),
        (tok_ref.at[pl.ds(0, 2)], halo_r.at[1]),
        (stage_e.at[1], halo_e.at[0]),
        (stage_e.at[0], halo_e.at[1]),
        (stage_c.at[3], halo_c.at[0]),
        (stage_c.at[2], halo_c.at[1]),
        (stage_c.at[1], halo_c.at[2]),
        (stage_c.at[0], halo_c.at[3]),
    )

    def halo_copy(i):
        way = WAYS[i]
        return pltpu.make_async_remote_copy(
            src_ref=moves[i][0], dst_ref=moves[i][1],
            send_sem=halo_send.at[i], recv_sem=halo_recv.at[i],
            device_id=at(mr + way[0], mc + way[1]), device_id_type=MESH,
        )

    def regroup(x, y, z, kinds):
        quarter = iota(x.shape, 1) // HEAD_DIM
        def choose(a, b, c, e):
            return jnp.where(quarter < 2, jnp.where(quarter == 0, a, b), jnp.where(quarter == 2, c, e))

        def turn(a, n):
            return pltpu.roll(a, n * HEAD_DIM, 1)

        makers = (
            lambda: choose(x, turn(x, 2), y, turn(z, 2)),
            lambda: choose(turn(x, 3), turn(y, 1), turn(y, 3), turn(z, 1)),
            lambda: choose(turn(x, 2), y, turn(z, 2), z),
        )
        return [(t, makers[t]()) for t in kinds]

    def order_weights(kinds):
        for i in range(n_chunk):
            native = [w_ref[:, (3 * i + t) * LANES : (3 * i + t + 1) * LANES] for t in range(3)]
            for t, tile in regroup(*native, kinds):
                wq[:, t * d + i * LANES : t * d + (i + 1) * LANES] = tile

    def put(ch, row, block):
        stag[ch, pl.ds(row * pitch + PAD, breadth), :] = block

    tokens = tok_ref[...].reshape(amount, d)

    def project(first, last):
        for p in range(first, last):
            y = dot(tokens, wq[:, p * PACK : (p + 1) * PACK])
            for c in range(PACK // LANES):
                for r in range(height):
                    put(2 * p + c, r + 2, y[r * breadth : (r + 1) * breadth, c * LANES : (c + 1) * LANES])

    fetch(1).wait()
    order_weights((1, 2))
    project(n_pack, 3 * n_pack)

    if paired:
        pl.semaphore_wait(barrier, n_all - 1)
    else:
        n_diag = sum(exists(way).astype(jnp.int32) for way in WAYS[4:])
        pl.semaphore_wait(barrier, n_rows - 1 + n_cols - 1 + n_diag)
    for i, way in enumerate(WAYS):
        @pl.when(exists(way))
        def _():
            halo_copy(i).start()

        @pl.when(jnp.logical_not(exists((-way[0], -way[1]))))
        def _():
            dst = moves[i][1]
            dst[...] = jnp.zeros(dst.shape, BF)


    prow, pcol = iota((PACK, PACK), 0), iota((PACK, PACK), 1)
    same = prow // HEAD_DIM == pcol // HEAD_DIM
    same_hot = one_hot(same)
    dn = (((0,), (0,)), ((), ()))

    def local_states(z, get_k, get_v):
        blank_rows = jnp.zeros((ROWS - HEAD_DIM - 1, PACK), F32)

        def piece(i):
            k = feature_map(get_k(i))
            st = lax.dot_general(k.astype(BF), get_v(i).astype(BF), dn, preferred_element_type=F32)
            st = jnp.sum(jnp.where(same, st, 0.0).reshape(8, HEAD_DIM, PACK), axis=0)
            return jnp.concatenate([st, jnp.sum(k, axis=0, keepdims=True), blank_rows], axis=0)

        if paired:
            part[z, 1 - side] = piece(1 - side)
            reduce_1(z)
            part[z, side] = piece(side)
        else:
            flat = jnp.concatenate([piece(i) for i in range(n_pack)], axis=1)
            step = ROWS // n_cols
            for q in range(n_cols):
                part[z, q] = flat[q * step : (q + 1) * step]
            reduce_1(z)

    side = lax.rem(mc, 2)
    half_cols = max(n_cols // 2, 1)
    n_chips = n_rows * half_cols if paired else 0
    slot = side if paired else mc
    ways = 2 if paired else n_cols

    n_far = n_chips if paired else n_rows
    per_hop = (ways - 1, n_far - 1, ways - 1, n_far - 1)

    def spot(z, hop, k):
        return z * sum(per_hop) + sum(per_hop[:hop]) + k - 1

    def rs_copy(z, k):
        peer = mc + 1 - 2 * side if paired else lax.rem(mc + k, n_cols)
        return pltpu.make_async_remote_copy(
            src_ref=part.at[z, 1 - side if paired else peer], dst_ref=rs.at[z, k - 1],
            send_sem=red_send.at[spot(z, 0, k)], recv_sem=red_recv.at[spot(z, 0, k)],
            device_id=at(mr, peer), device_id_type=MESH,
        )

    def far_device(k):
        if paired:
            chip = lax.rem(mr * half_cols + mc // 2 + k, n_chips)
            device = at(chip // half_cols, 2 * lax.rem(chip, half_cols) + side)
        else:
            device = at(lax.rem(mr + k, n_rows), mc)
        return device

    def ar_copy(z, k):
        return pltpu.make_async_remote_copy(
            src_ref=ar_src.at[z], dst_ref=ar.at[z, k - 1],
            send_sem=red_send.at[spot(z, 1, k)], recv_sem=red_recv.at[spot(z, 1, k)],
            device_id=far_device(k), device_id_type=MESH,
        )

    def tot_copy(z, k):
        return pltpu.make_async_remote_copy(
            src_ref=tot_src.at[z], dst_ref=tots.at[z, k - 1],
            send_sem=red_send.at[spot(z, 3, k)], recv_sem=red_recv.at[spot(z, 3, k)],
            device_id=far_device(k), device_id_type=MESH,
        )

    def ag_copy(z, k, back=False):
        if paired:
            peer, other = mc + 1 - 2 * side, 1 - side
        else:
            peer = other = lax.rem(mc + (n_cols - k if back else k), n_cols)
        return pltpu.make_async_remote_copy(
            src_ref=ag.at[z, slot], dst_ref=ag.at[z, other if back else slot],
            send_sem=red_send.at[spot(z, 2, k)], recv_sem=red_recv.at[spot(z, 2, k)],
            device_id=at(mr, peer), device_id_type=MESH,
        )

    def reduce_1(z):
        for k in range(1, ways):
            rs_copy(z, k).start()

    def reduce_2(z):
        total = part[z, slot]
        for k in range(1, ways):
            rs_copy(z, k).wait_recv()
            total = total + rs[z, k - 1]
        if paired:
            ar_src[z] = total[:HEAD_DIM].astype(BF)
            tot_src[z] = total[HEAD_DIM : HEAD_DIM + 1]
        else:
            ar_src[z] = total
        for k in range(1, n_far):
            ar_copy(z, k).start()
            if paired:
                tot_copy(z, k).start()

    def reduce_3(z):
        total = ar_src[z].astype(F32)
        tot = tot_src[z]
        for k in range(1, n_far):
            ar_copy(z, k).wait_recv()
            total = total + ar[z, k - 1].astype(F32)
            if paired:
                tot_copy(z, k).wait_recv()
                tot = tot + tots[z, k - 1]
        if paired:
            total = jnp.concatenate([total, tot, jnp.zeros((ROWS - HEAD_DIM - 1, PACK), F32)], axis=0)
        ag[z, slot] = total
        for k in range(1, ways):
            ag_copy(z, k).start()

    def reduce_4(z):
        for k in range(1, ways):
            ag_copy(z, k, back=True).wait_recv()
        return jnp.concatenate([ag[z, q] for q in range(ways)], axis=1 if paired else 0)

    def conv(first, last, start_row, n_lines, hop, count):
        def chunk(ch, _):
            w = [jnp.broadcast_to(taps[ch, t : t + 1, :], (SUB, LANES)).astype(BF) for t in range(25)]

            def lines(q, _):
                r0 = start_row + q * hop
                sums = [[None] * inner for _ in range(n_lines)]
                for rr in range(n_lines + 4):
                    start = (r0 + rr) * pitch + PAD - 2
                    xs = [stag[ch, pl.ds(start + jj, SUB, stride=inner), :].astype(BF) for jj in range(wide)]
                    for n in range(n_lines):
                        a = rr - n
                        if 0 <= a < 5:
                            for j in range(inner):
                                term = xs[j] * w[5 * a]
                                for b in range(1, 5):
                                    term = term + xs[j + b] * w[5 * a + b]
                                sums[n][j] = term if a == 0 else sums[n][j] + term
                for n in range(n_lines):
                    for j in range(inner):
                        spread[ch, pl.ds((r0 + n) * breadth + j, SUB, stride=inner), :] = sums[n][j].astype(F32)
                return 0

            lax.fori_loop(0, count, lines, 0)
            return 0

        lax.fori_loop(first, last, chunk, 0)

    def native(t, i):
        lo = t * n_chunk + i * (PACK // LANES)
        return jnp.concatenate(
            [
                jnp.concatenate([stag[lo + c, pl.ds((r + 2) * pitch + PAD, breadth), :] for r in range(height)], axis=0)
                for c in range(PACK // LANES)
            ],
            axis=1,
        )

    def grouped(t, i):
        lo = t * n_chunk + i * (PACK // LANES)
        x = jnp.concatenate([spread[lo + c].astype(BF) for c in range(PACK // LANES)], axis=1)
        return dot(x, gbd[t * n_pack + i])

    def mix_states(z, flat):
        for i in range(n_pack):
            rows = slice(z * d + i * PACK, z * d + (i + 1) * PACK)
            st = flat[:HEAD_DIM, i * PACK : (i + 1) * PACK]
            st = jnp.where(same, jnp.concatenate([st] * 8, axis=0), 0.0).astype(BF)
            mix[i * PACK : (i + 1) * PACK, :] = (dot(st, pw_ref[rows, :]) * gain_ref[...]).astype(BF)

    def attend(flat, get_q):
        heads = []
        for i in range(n_pack):
            tot = flat[HEAD_DIM : HEAD_DIM + 1, i * PACK : (i + 1) * PACK]
            q = get_q(i)
            den = dot((q * tot).astype(BF), same_hot)
            heads.append((q * pl.reciprocal(den, approx=True)).astype(BF))
        return dot(jnp.concatenate(heads, axis=1), mix[...])

    local_states(0, lambda i: native(1, i), lambda i: native(2, i))
    def order_taps(kinds):
        for i in range(n_chunk):
            native_taps = [dk_ref[:, (3 * i + t) * LANES : (3 * i + t + 1) * LANES] for t in range(3)]
            for t, tile in regroup(*native_taps, kinds):
                taps[t * n_chunk + i, :25, :] = tile

    n_group = gk_ref.shape[2]
    heads_each = n_group // 3
    quarter = iota((heads_each, LANES), 1) // HEAD_DIM
    own = iota((LANES, LANES), 0) // HEAD_DIM == iota((LANES, LANES), 1) // HEAD_DIM
    blank = jnp.zeros((LANES, LANES), BF)

    def order_groups(kinds):
        flat_gk = gk_ref[...].reshape(HEAD_DIM * HEAD_DIM, n_group)
        for t in kinds:
            pick = one_hot(3 * iota((heads_each, n_group), 0) + t == iota((heads_each, n_group), 1))
            turned = lax.dot_general(pick, flat_gk, (((1,), (1,)), ((), ())), preferred_element_type=F32)
            for k in range(HEAD_DIM * HEAD_DIM // LANES):
                tile = turned[:, k * LANES : (k + 1) * LANES]
                turns = [tile] + [pltpu.roll(tile, n * HEAD_DIM, 1) for n in range(1, 4)]
                for j in range(4):
                    t0, t1, t2, t3 = (turns[(b - j) % 4] for b in range(4))
                    copy = jnp.where(quarter < 2, jnp.where(quarter == 0, t0, t1), jnp.where(quarter == 2, t2, t3))
                    gsq[pl.ds(t * d + 4 * k + j, heads_each, stride=HEAD_DIM), :] = copy
            for i in range(n_pack):
                blocks = []
                for c in range(PACK // LANES):
                    block = gsq[t * d + (2 * i + c) * LANES : t * d + (2 * i + c + 1) * LANES, :]
                    blocks.append(jnp.where(own, block, 0.0).astype(BF))
                gbd[t * n_pack + i, :LANES, :] = jnp.concatenate([blocks[0], blank], axis=1)
                gbd[t * n_pack + i, LANES:, :] = jnp.concatenate([blank, blocks[1]], axis=1)

    def arrived(which):
        for i in which:
            way = WAYS[i]

            @pl.when(exists((-way[0], -way[1])))
            def _():
                halo_copy(i).wait_recv()

    def project_sides(first, last, repair=False):
        around = halo_e[...].reshape(2 * e, d)
        for p in range(first, last):
            y = dot(around, wq[:, p * PACK : (p + 1) * PACK])
            for c in range(PACK // LANES):
                for side in range(2):
                    for b in range(2):
                        col = (breadth + PAD if side else PAD - 2) + b
                        lo = side * e + b * height
                        stag[2 * p + c, pl.ds(2 * pitch + col, height, stride=pitch), :] = (
                            y[lo : lo + height, c * LANES : (c + 1) * LANES])
                if repair:
                    repair_rows(2 * p + c, y[:, c * LANES : (c + 1) * LANES])

    def repair_rows(ch, y):
        n = height - 4

        def part_sum(side, terms):
            total = None
            for b, tap in terms:
                for a in range(5):
                    lo = side * e + b * height + a
                    term = y[lo : lo + n] * taps[ch, 5 * a + tap : 5 * a + tap + 1, :]
                    total = term if total is None else total + term
            return total

        for col, side, terms in (
            (0, 0, ((0, 0), (1, 1))),
            (1, 0, ((1, 0),)),
            (breadth - 2, 1, ((0, 4),)),
            (breadth - 1, 1, ((0, 3), (1, 4))),
        ):
            rows = pl.ds(2 * breadth + col, n, stride=breadth)
            spread[ch, rows, :] = spread[ch, rows, :] + part_sum(side, terms)

    def project_rows(first, last):
        around = jnp.concatenate([halo_r[...].reshape(4 * breadth, d), halo_c[...].reshape(4 * SUB, d)], axis=0)
        for p in range(first, last):
            y = dot(around, wq[:, p * PACK : (p + 1) * PACK])
            for c in range(PACK // LANES):
                ch = 2 * p + c
                cut = y[:, c * LANES : (c + 1) * LANES]
                for n, row in enumerate((0, 1, height + 2, height + 3)):
                    put(ch, row, cut[n * breadth : (n + 1) * breadth])
                for side in range(2):
                    for b in range(2):
                        col = (breadth + PAD if side else PAD - 2) + b
                        for n in range(2):
                            lo = 4 * breadth + (2 * n + side) * SUB + 2 * b
                            row = n * (height + 2)
                            stag[ch, pl.ds(row * pitch + col, 2, stride=pitch), :] = cut[lo : lo + 2]

    fetch(2).wait()
    order_taps((1, 2))
    fetch(3).wait()
    order_groups((1, 2))
    reduce_2(0)
    gap = jnp.zeros((PAD, LANES), F32)
    for ch in range(n_chunk, 3 * n_chunk):
        for r in range(2, height + 2):
            stag[ch, r * pitch : r * pitch + PAD, :] = gap
            stag[ch, r * pitch + PAD + breadth : (r + 1) * pitch, :] = gap
    conv(n_chunk, 3 * n_chunk, 2, LINES, LINES, (height - 4) // LINES)
    arrived((2, 3))
    project_sides(n_pack, 3 * n_pack, repair=True)
    arrived((0, 1, 4, 5, 6, 7))
    project_rows(n_pack, 3 * n_pack)
    conv(n_chunk, 3 * n_chunk, 0, 2, height - 2, 2)
    local_states(1, lambda i: grouped(1, i), lambda i: grouped(2, i))
    order_weights((0,))
    reduce_2(1)
    project(0, n_pack)
    order_taps((0,))
    order_groups((0,))
    reduce_3(0)
    project_sides(0, n_pack)
    project_rows(0, n_pack)
    whole = (0, LINES, LINES, height // LINES)
    conv(0, n_chunk, *whole)
    for i in range(4, 7):
        fetch(i).wait()
    flat = reduce_4(0)
    mix_states(0, flat)
    acc[...] = attend(flat, lambda i: feature_map(native(0, i))) + (tokens.astype(F32) + bias_ref[...])
    reduce_3(1)
    for i in range(n_pack):
        q = feature_map(grouped(0, i))
        for c in range(PACK // LANES):
            spread[2 * i + c] = q[:, c * LANES : (c + 1) * LANES]
    flat = reduce_4(1)
    mix_states(1, flat)
    n_part = 2
    piece = height // n_part

    for b in range(n_part):
        cut = slice(b * piece * breadth, (b + 1) * piece * breadth)
        late = [
            jnp.concatenate([spread[2 * i + c, cut] for c in range(PACK // LANES)], axis=1) for i in range(n_pack)
        ]
        got = acc[cut] + attend(flat, lambda i: late[i])
        out_ref[b * piece : (b + 1) * piece] = got.astype(BF).reshape(piece, breadth, d)

    for i, way in enumerate(WAYS):
        @pl.when(exists(way))
        def _():
            halo_copy(i).wait_send()
    for z in range(2):
        for k in range(1, ways):
            rs_copy(z, k).wait_send()
            ag_copy(z, k).wait_send()
        for k in range(1, n_far):
            ar_copy(z, k).wait_send()
            if paired:
                tot_copy(z, k).wait_send()


def finish(src, out, sem):
    copy = pltpu.make_async_copy(src, out, sem)
    copy.start()
    copy.wait()


def body(n_rows, n_cols, tokens, qkv_weight, depth_kernel, group_kernel, proj_weight, out_gain, out_bias):
    height, breadth, d = tokens.shape
    paired = is_paired(n_rows, n_cols, d)
    ways, far = (2, n_rows * n_cols // 2) if paired else (n_cols, n_rows)
    block = (ROWS, PACK) if paired else (ROWS // n_cols, d)
    far_block, far_type = ((HEAD_DIM, PACK), BF) if paired else (block, F32)
    most = 4 * max(ways + far - 2, 1)
    operands = (
        tokens, qkv_weight, depth_kernel, jnp.transpose(group_kernel, (1, 2, 0)), proj_weight, out_gain[None, :], out_bias[None, :])
    operands = [pltpu.with_memory_space_constraint(x, pltpu.HBM) for x in operands]
    mixed = pl.pallas_call(
        functools.partial(kernel, n_rows, n_cols),
        out_shape=pltpu.VMEM((height, breadth, d), BF),
        in_specs=[pl.BlockSpec(memory_space=pl.ANY)] * 7,
        out_specs=pl.BlockSpec(memory_space=pltpu.VMEM),
        scratch_shapes=[pltpu.VMEM(x.shape, x.dtype) for x in operands] + [
            pltpu.VMEM((2, 2 * height, d), BF),
            pltpu.VMEM((4, SUB, d), BF),
            pltpu.VMEM((2, 2 * height, d), BF),
            pltpu.VMEM((4, SUB, d), BF),
            pltpu.VMEM((2, 2, breadth, d), BF),
            pltpu.VMEM((d, 3 * d), BF),
            pltpu.VMEM((3 * d // LANES, 32, LANES), F32),
            pltpu.VMEM((3 * d, LANES), F32),
            pltpu.VMEM((3 * d // PACK, PACK, PACK), BF),
            pltpu.VMEM((3 * d // LANES, (height + 4) * (breadth + 2 * PAD), LANES), F32),
            pltpu.VMEM((3 * d // LANES, height * breadth, LANES), F32),
            pltpu.VMEM((height * breadth, d), F32),
            pltpu.VMEM((d, d), BF),
            pltpu.VMEM((2, ways, *block), F32),
            pltpu.VMEM((2, ways - 1, *block), F32),
            pltpu.VMEM((2, *far_block), far_type),
            pltpu.VMEM((2, far - 1, *far_block), far_type),
            pltpu.VMEM((2, 1, PACK), F32),
            pltpu.VMEM((2, far - 1, 1, PACK), F32),
            pltpu.VMEM((2, ways, *block), F32),
            pltpu.SemaphoreType.DMA((8,)),
            pltpu.SemaphoreType.DMA((8,)),
            pltpu.SemaphoreType.DMA((most,)),
            pltpu.SemaphoreType.DMA((most,)),
            pltpu.SemaphoreType.DMA((7,)),
        ],
        compiler_params=pltpu.CompilerParams(
            collective_id=0, has_side_effects=True, vmem_limit_bytes=48 * 1024 * 1024
        ),
        name="attention_module",
    )(*operands)
    return pl.pallas_call(
        finish,
        out_shape=jax.ShapeDtypeStruct((height, breadth, d), BF),
        in_specs=[pl.BlockSpec(memory_space=pl.ANY)],
        out_specs=pl.BlockSpec(memory_space=pl.ANY),
        scratch_shapes=[pltpu.SemaphoreType.DMA],
        compiler_params=pltpu.CompilerParams(vmem_limit_bytes=4 * 1024 * 1024),
        name="finish",
    )(mixed)


def solution(mesh):
    placed = (P(("groups", "rows"), "cols", None), P(), P(), P(), P(), P(), P())
    return jax.shard_map(
        functools.partial(body, mesh.shape["rows"], mesh.shape["cols"]),
        mesh=mesh,
        in_specs=placed,
        out_specs=P(("groups", "rows"), "cols", None),
        check_vma=False,
    )
```

```python
import functools

import jax
import jax.numpy as jnp
from jax import lax
from jax.experimental import pallas as pl
from jax.experimental.pallas import tpu as pltpu
from jax.sharding import PartitionSpec as P

HEAD_DIM = 32
PACK = 8 * HEAD_DIM
LANES = 128
SUB = 16
PAD = 8
LINES = 4
ROWS = HEAD_DIM + 8
BF = jnp.bfloat16
F32 = jnp.float32
WAYS = ((1, 0), (-1, 0), (0, 1), (0, -1), (1, 1), (1, -1), (-1, 1), (-1, -1))


def is_paired(n_rows, n_cols, d):
    return n_cols % 2 == 0 and n_rows * n_cols <= 32 and d == 2 * PACK


def iota(shape, dim):
    return lax.broadcasted_iota(jnp.int32, shape, dim)


def dot(a, b):
    return jnp.dot(a, b, preferred_element_type=F32)


def feature_map(u):
    return jnp.where(u > 0, u + 1.0, jnp.exp(jnp.minimum(u, 0.0)))


def one_hot(mask):
    return jnp.where(mask, 1.0, 0.0).astype(BF)


def kernel(
    n_rows, n_cols,
    *refs,
):
    sources, out_ref, refs = refs[:7], refs[7], refs[8:]
    inputs, refs = refs[:7], refs[7:]
    tok_ref, w_ref, dk_ref, gk_ref, pw_ref, gain_ref, bias_ref = inputs
    (
    stage_e, stage_c, halo_e, halo_c, halo_r, wq, taps, gsq, gbd, stag, spread, acc, mix,
    part, rs, ar_src, ar, tot_src, tots, ag,
    halo_send, halo_recv, red_send, red_recv, load,
    ) = refs

    def fetch(i):
        return pltpu.make_async_copy(sources[i], inputs[i], load.at[i])

    for i in range(2):
        fetch(i).start()
    height, breadth, d = tok_ref.shape
    inner = breadth // SUB
    wide = inner + 4
    amount = height * breadth
    n_pack = d // PACK
    n_chunk = d // LANES
    pitch = breadth + 2 * PAD
    mr, mc = lax.axis_index("rows"), lax.axis_index("cols")

    def exists(way):
        r, c = mr + way[0], mc + way[1]
        return (r >= 0) & (r < n_rows) & (c >= 0) & (c < n_cols)

    def at(r, c):
        return {"rows": r, "cols": c}

    MESH = pl.DeviceIdType.MESH
    barrier = pltpu.get_barrier_semaphore()
    n_all = n_rows * n_cols
    paired = is_paired(n_rows, n_cols, d)
    me = mr * n_cols + mc
    if paired:
        for k in range(1, n_all):
            peer = lax.rem(me + k, n_all)
            pl.semaphore_signal(
                barrier, inc=1, device_id=at(peer // n_cols, lax.rem(peer, n_cols)), device_id_type=MESH)
    else:
        for k in range(1, n_rows):
            pl.semaphore_signal(barrier, inc=1, device_id=at(lax.rem(mr + k, n_rows), mc), device_id_type=MESH)
        for k in range(1, n_cols):
            pl.semaphore_signal(barrier, inc=1, device_id=at(mr, lax.rem(mc + k, n_cols)), device_id_type=MESH)
        for way in WAYS[4:]:
            @pl.when(exists(way))
            def _():
                pl.semaphore_signal(barrier, inc=1, device_id=at(mr + way[0], mc + way[1]), device_id_type=MESH)

    fetch(0).wait()
    e = 2 * height
    rows_out = 2 * e + 4 * SUB
    m = iota((rows_out, amount), 0)
    src = iota((rows_out, amount), 1)
    right = (m >= e).astype(jnp.int32)
    me_ = m - right * e
    edge = (me_ % height) * breadth + me_ // height + right * (breadth - 2)
    cm = m - 2 * e
    ci, cr = cm // SUB, cm % SUB
    corner = ((cr % 2) + (ci // 2) * (height - 2)) * breadth + (cr // 2) + (ci % 2) * (breadth - 2)
    want = jnp.where(m < 2 * e, edge, jnp.where(cr < 4, corner, -1))
    sel = dot(one_hot(want == src), tok_ref[...].reshape(amount, d)).astype(BF)
    stage_e[...] = sel[: 2 * e].reshape(2, e, d)
    stage_c[...] = sel[2 * e :].reshape(4, SUB, d)

    moves = (
        (tok_ref.at[pl.ds(height - 2, 2)], halo_r.at[0]),
        (tok_ref.at[pl.ds(0, 2)], halo_r.at[1]),
        (stage_e.at[1], halo_e.at[0]),
        (stage_e.at[0], halo_e.at[1]),
        (stage_c.at[3], halo_c.at[0]),
        (stage_c.at[2], halo_c.at[1]),
        (stage_c.at[1], halo_c.at[2]),
        (stage_c.at[0], halo_c.at[3]),
    )

    def halo_copy(i):
        way = WAYS[i]
        return pltpu.make_async_remote_copy(
            src_ref=moves[i][0], dst_ref=moves[i][1],
            send_sem=halo_send.at[i], recv_sem=halo_recv.at[i],
            device_id=at(mr + way[0], mc + way[1]), device_id_type=MESH,
        )

    def regroup(x, y, z, kinds):
        quarter = iota(x.shape, 1) // HEAD_DIM
        def choose(a, b, c, e):
            return jnp.where(quarter < 2, jnp.where(quarter == 0, a, b), jnp.where(quarter == 2, c, e))

        def turn(a, n):
            return pltpu.roll(a, n * HEAD_DIM, 1)

        makers = (
            lambda: choose(x, turn(x, 2), y, turn(z, 2)),
            lambda: choose(turn(x, 3), turn(y, 1), turn(y, 3), turn(z, 1)),
            lambda: choose(turn(x, 2), y, turn(z, 2), z),
        )
        return [(t, makers[t]()) for t in kinds]

    def order_weights(kinds):
        for i in range(n_chunk):
            native = [w_ref[:, (3 * i + t) * LANES : (3 * i + t + 1) * LANES] for t in range(3)]
            for t, tile in regroup(*native, kinds):
                wq[:, t * d + i * LANES : t * d + (i + 1) * LANES] = tile

    def put(ch, row, block):
        stag[ch, pl.ds(row * pitch + PAD, breadth), :] = block

    tokens = tok_ref[...].reshape(amount, d)

    def project(first, last):
        for p in range(first, last):
            y = dot(tokens, wq[:, p * PACK : (p + 1) * PACK])
            for c in range(PACK // LANES):
                for r in range(height):
                    put(2 * p + c, r + 2, y[r * breadth : (r + 1) * breadth, c * LANES : (c + 1) * LANES])

    fetch(1).wait()
    for i in range(2, 7):
        fetch(i).start()
    order_weights((1, 2))
    project(n_pack, 3 * n_pack)

    if paired:
        pl.semaphore_wait(barrier, n_all - 1)
    else:
        n_diag = sum(exists(way).astype(jnp.int32) for way in WAYS[4:])
        pl.semaphore_wait(barrier, n_rows - 1 + n_cols - 1 + n_diag)
    for i, way in enumerate(WAYS):
        @pl.when(exists(way))
        def _():
            halo_copy(i).start()

        @pl.when(jnp.logical_not(exists((-way[0], -way[1]))))
        def _():
            dst = moves[i][1]
            dst[...] = jnp.zeros(dst.shape, BF)


    prow, pcol = iota((PACK, PACK), 0), iota((PACK, PACK), 1)
    same = prow // HEAD_DIM == pcol // HEAD_DIM
    same_hot = one_hot(same)
    dn = (((0,), (0,)), ((), ()))

    def local_states(z, get_k, get_v):
        blank_rows = jnp.zeros((ROWS - HEAD_DIM - 1, PACK), F32)

        def piece(i):
            k = feature_map(get_k(i))
            st = lax.dot_general(k.astype(BF), get_v(i).astype(BF), dn, preferred_element_type=F32)
            st = jnp.sum(jnp.where(same, st, 0.0).reshape(8, HEAD_DIM, PACK), axis=0)
            return jnp.concatenate([st, jnp.sum(k, axis=0, keepdims=True), blank_rows], axis=0)

        if paired:
            part[z, 1 - side] = piece(1 - side)
            reduce_1(z)
            part[z, side] = piece(side)
        else:
            flat = jnp.concatenate([piece(i) for i in range(n_pack)], axis=1)
            step = ROWS // n_cols
            for q in range(n_cols):
                part[z, q] = flat[q * step : (q + 1) * step]
            reduce_1(z)

    side = lax.rem(mc, 2)
    half_cols = max(n_cols // 2, 1)
    n_chips = n_rows * half_cols if paired else 0
    slot = side if paired else mc
    ways = 2 if paired else n_cols

    n_far = n_chips if paired else n_rows
    per_hop = (ways - 1, n_far - 1, ways - 1, n_far - 1)

    def spot(z, hop, k):
        return z * sum(per_hop) + sum(per_hop[:hop]) + k - 1

    def rs_copy(z, k):
        peer = mc + 1 - 2 * side if paired else lax.rem(mc + k, n_cols)
        return pltpu.make_async_remote_copy(
            src_ref=part.at[z, 1 - side if paired else peer], dst_ref=rs.at[z, k - 1],
            send_sem=red_send.at[spot(z, 0, k)], recv_sem=red_recv.at[spot(z, 0, k)],
            device_id=at(mr, peer), device_id_type=MESH,
        )

    def far_device(k):
        if paired:
            chip = lax.rem(mr * half_cols + mc // 2 + k, n_chips)
            device = at(chip // half_cols, 2 * lax.rem(chip, half_cols) + side)
        else:
            device = at(lax.rem(mr + k, n_rows), mc)
        return device

    def ar_copy(z, k):
        return pltpu.make_async_remote_copy(
            src_ref=ar_src.at[z], dst_ref=ar.at[z, k - 1],
            send_sem=red_send.at[spot(z, 1, k)], recv_sem=red_recv.at[spot(z, 1, k)],
            device_id=far_device(k), device_id_type=MESH,
        )

    def tot_copy(z, k):
        return pltpu.make_async_remote_copy(
            src_ref=tot_src.at[z], dst_ref=tots.at[z, k - 1],
            send_sem=red_send.at[spot(z, 3, k)], recv_sem=red_recv.at[spot(z, 3, k)],
            device_id=far_device(k), device_id_type=MESH,
        )

    def ag_copy(z, k, back=False):
        if paired:
            peer, other = mc + 1 - 2 * side, 1 - side
        else:
            peer = other = lax.rem(mc + (n_cols - k if back else k), n_cols)
        return pltpu.make_async_remote_copy(
            src_ref=ag.at[z, slot], dst_ref=ag.at[z, other if back else slot],
            send_sem=red_send.at[spot(z, 2, k)], recv_sem=red_recv.at[spot(z, 2, k)],
            device_id=at(mr, peer), device_id_type=MESH,
        )

    def reduce_1(z):
        for k in range(1, ways):
            rs_copy(z, k).start()

    def reduce_2(z):
        total = part[z, slot]
        for k in range(1, ways):
            rs_copy(z, k).wait_recv()
            total = total + rs[z, k - 1]
        if paired:
            ar_src[z] = total[:HEAD_DIM].astype(BF)
            tot_src[z] = total[HEAD_DIM : HEAD_DIM + 1]
        else:
            ar_src[z] = total
        for k in range(1, n_far):
            ar_copy(z, k).start()
            if paired:
                tot_copy(z, k).start()

    def reduce_3(z):
        total = ar_src[z].astype(F32)
        tot = tot_src[z]
        for k in range(1, n_far):
            ar_copy(z, k).wait_recv()
            total = total + ar[z, k - 1].astype(F32)
            if paired:
                tot_copy(z, k).wait_recv()
                tot = tot + tots[z, k - 1]
        if paired:
            total = jnp.concatenate([total, tot, jnp.zeros((ROWS - HEAD_DIM - 1, PACK), F32)], axis=0)
        ag[z, slot] = total
        for k in range(1, ways):
            ag_copy(z, k).start()

    def reduce_4(z):
        for k in range(1, ways):
            ag_copy(z, k, back=True).wait_recv()
        return jnp.concatenate([ag[z, q] for q in range(ways)], axis=1 if paired else 0)

    def conv(first, last, start_row, n_lines, hop, count):
        def chunk(ch, _):
            w = [jnp.broadcast_to(taps[ch, t : t + 1, :], (SUB, LANES)).astype(BF) for t in range(25)]

            def lines(q, _):
                r0 = start_row + q * hop
                sums = [[None] * inner for _ in range(n_lines)]
                for rr in range(n_lines + 4):
                    start = (r0 + rr) * pitch + PAD - 2
                    xs = [stag[ch, pl.ds(start + jj, SUB, stride=inner), :].astype(BF) for jj in range(wide)]
                    for n in range(n_lines):
                        a = rr - n
                        if 0 <= a < 5:
                            for j in range(inner):
                                term = xs[j] * w[5 * a]
                                for b in range(1, 5):
                                    term = term + xs[j + b] * w[5 * a + b]
                                sums[n][j] = term if a == 0 else sums[n][j] + term
                for n in range(n_lines):
                    for j in range(inner):
                        spread[ch, pl.ds((r0 + n) * breadth + j, SUB, stride=inner), :] = sums[n][j].astype(F32)
                return 0

            lax.fori_loop(0, count, lines, 0)
            return 0

        lax.fori_loop(first, last, chunk, 0)

    def native(t, i):
        lo = t * n_chunk + i * (PACK // LANES)
        return jnp.concatenate(
            [
                jnp.concatenate([stag[lo + c, pl.ds((r + 2) * pitch + PAD, breadth), :] for r in range(height)], axis=0)
                for c in range(PACK // LANES)
            ],
            axis=1,
        )

    def grouped(t, i):
        lo = t * n_chunk + i * (PACK // LANES)
        x = jnp.concatenate([spread[lo + c].astype(BF) for c in range(PACK // LANES)], axis=1)
        return dot(x, gbd[t * n_pack + i])

    def mix_states(z, flat):
        for i in range(n_pack):
            rows = slice(z * d + i * PACK, z * d + (i + 1) * PACK)
            st = flat[:HEAD_DIM, i * PACK : (i + 1) * PACK]
            st = jnp.where(same, jnp.concatenate([st] * 8, axis=0), 0.0).astype(BF)
            mix[i * PACK : (i + 1) * PACK, :] = (dot(st, pw_ref[rows, :]) * gain_ref[...]).astype(BF)

    def attend(flat, get_q):
        heads = []
        for i in range(n_pack):
            tot = flat[HEAD_DIM : HEAD_DIM + 1, i * PACK : (i + 1) * PACK]
            q = get_q(i)
            den = dot((q * tot).astype(BF), same_hot)
            heads.append((q * pl.reciprocal(den, approx=True)).astype(BF))
        return dot(jnp.concatenate(heads, axis=1), mix[...])

    local_states(0, lambda i: native(1, i), lambda i: native(2, i))
    def order_taps(kinds):
        for i in range(n_chunk):
            native_taps = [dk_ref[:, (3 * i + t) * LANES : (3 * i + t + 1) * LANES] for t in range(3)]
            for t, tile in regroup(*native_taps, kinds):
                taps[t * n_chunk + i, :25, :] = tile

    n_group = gk_ref.shape[2]
    heads_each = n_group // 3
    quarter = iota((heads_each, LANES), 1) // HEAD_DIM
    own = iota((LANES, LANES), 0) // HEAD_DIM == iota((LANES, LANES), 1) // HEAD_DIM
    blank = jnp.zeros((LANES, LANES), BF)

    def order_groups(kinds):
        flat_gk = gk_ref[...].reshape(HEAD_DIM * HEAD_DIM, n_group)
        for t in kinds:
            pick = one_hot(3 * iota((heads_each, n_group), 0) + t == iota((heads_each, n_group), 1))
            turned = lax.dot_general(pick, flat_gk, (((1,), (1,)), ((), ())), preferred_element_type=F32)
            for k in range(HEAD_DIM * HEAD_DIM // LANES):
                tile = turned[:, k * LANES : (k + 1) * LANES]
                turns = [tile] + [pltpu.roll(tile, n * HEAD_DIM, 1) for n in range(1, 4)]
                for j in range(4):
                    t0, t1, t2, t3 = (turns[(b - j) % 4] for b in range(4))
                    copy = jnp.where(quarter < 2, jnp.where(quarter == 0, t0, t1), jnp.where(quarter == 2, t2, t3))
                    gsq[pl.ds(t * d + 4 * k + j, heads_each, stride=HEAD_DIM), :] = copy
            for i in range(n_pack):
                blocks = []
                for c in range(PACK // LANES):
                    block = gsq[t * d + (2 * i + c) * LANES : t * d + (2 * i + c + 1) * LANES, :]
                    blocks.append(jnp.where(own, block, 0.0).astype(BF))
                gbd[t * n_pack + i, :LANES, :] = jnp.concatenate([blocks[0], blank], axis=1)
                gbd[t * n_pack + i, LANES:, :] = jnp.concatenate([blank, blocks[1]], axis=1)

    def arrived(which):
        for i in which:
            way = WAYS[i]

            @pl.when(exists((-way[0], -way[1])))
            def _():
                halo_copy(i).wait_recv()

    def project_sides(first, last, repair=False):
        around = halo_e[...].reshape(2 * e, d)
        for p in range(first, last):
            y = dot(around, wq[:, p * PACK : (p + 1) * PACK])
            for c in range(PACK // LANES):
                for side in range(2):
                    for b in range(2):
                        col = (breadth + PAD if side else PAD - 2) + b
                        lo = side * e + b * height
                        stag[2 * p + c, pl.ds(2 * pitch + col, height, stride=pitch), :] = (
                            y[lo : lo + height, c * LANES : (c + 1) * LANES])
                if repair:
                    repair_rows(2 * p + c, y[:, c * LANES : (c + 1) * LANES])

    def repair_rows(ch, y):
        n = height - 4

        def part_sum(side, terms):
            total = None
            for b, tap in terms:
                for a in range(5):
                    lo = side * e + b * height + a
                    term = y[lo : lo + n] * taps[ch, 5 * a + tap : 5 * a + tap + 1, :]
                    total = term if total is None else total + term
            return total

        for col, side, terms in (
            (0, 0, ((0, 0), (1, 1))),
            (1, 0, ((1, 0),)),
            (breadth - 2, 1, ((0, 4),)),
            (breadth - 1, 1, ((0, 3), (1, 4))),
        ):
            rows = pl.ds(2 * breadth + col, n, stride=breadth)
            spread[ch, rows, :] = spread[ch, rows, :] + part_sum(side, terms)

    def project_rows(first, last):
        around = jnp.concatenate([halo_r[...].reshape(4 * breadth, d), halo_c[...].reshape(4 * SUB, d)], axis=0)
        for p in range(first, last):
            y = dot(around, wq[:, p * PACK : (p + 1) * PACK])
            for c in range(PACK // LANES):
                ch = 2 * p + c
                cut = y[:, c * LANES : (c + 1) * LANES]
                for n, row in enumerate((0, 1, height + 2, height + 3)):
                    put(ch, row, cut[n * breadth : (n + 1) * breadth])
                for side in range(2):
                    for b in range(2):
                        col = (breadth + PAD if side else PAD - 2) + b
                        for n in range(2):
                            lo = 4 * breadth + (2 * n + side) * SUB + 2 * b
                            row = n * (height + 2)
                            stag[ch, pl.ds(row * pitch + col, 2, stride=pitch), :] = cut[lo : lo + 2]

    fetch(2).wait()
    order_taps((1, 2))
    fetch(3).wait()
    order_groups((1, 2))
    reduce_2(0)
    gap = jnp.zeros((PAD, LANES), F32)
    for ch in range(n_chunk, 3 * n_chunk):
        for r in range(2, height + 2):
            stag[ch, r * pitch : r * pitch + PAD, :] = gap
            stag[ch, r * pitch + PAD + breadth : (r + 1) * pitch, :] = gap
    conv(n_chunk, 3 * n_chunk, 2, LINES, LINES, (height - 4) // LINES)
    arrived((2, 3))
    project_sides(n_pack, 3 * n_pack, repair=True)
    arrived((0, 1, 4, 5, 6, 7))
    project_rows(n_pack, 3 * n_pack)
    conv(n_chunk, 3 * n_chunk, 0, 2, height - 2, 2)
    local_states(1, lambda i: grouped(1, i), lambda i: grouped(2, i))
    order_weights((0,))
    reduce_2(1)
    project(0, n_pack)
    order_taps((0,))
    order_groups((0,))
    reduce_3(0)
    project_sides(0, n_pack)
    project_rows(0, n_pack)
    whole = (0, LINES, LINES, height // LINES)
    conv(0, n_chunk, *whole)
    for i in range(4, 7):
        fetch(i).wait()
    flat = reduce_4(0)
    mix_states(0, flat)
    acc[...] = attend(flat, lambda i: feature_map(native(0, i))) + (tokens.astype(F32) + bias_ref[...])
    reduce_3(1)
    for i in range(n_pack):
        q = feature_map(grouped(0, i))
        for c in range(PACK // LANES):
            spread[2 * i + c] = q[:, c * LANES : (c + 1) * LANES]
    flat = reduce_4(1)
    mix_states(1, flat)
    n_part = 2
    piece = height // n_part

    for b in range(n_part):
        cut = slice(b * piece * breadth, (b + 1) * piece * breadth)
        late = [
            jnp.concatenate([spread[2 * i + c, cut] for c in range(PACK // LANES)], axis=1) for i in range(n_pack)
        ]
        got = acc[cut] + attend(flat, lambda i: late[i])
        out_ref[b * piece : (b + 1) * piece] = got.astype(BF).reshape(piece, breadth, d)

    for i, way in enumerate(WAYS):
        @pl.when(exists(way))
        def _():
            halo_copy(i).wait_send()
    for z in range(2):
        for k in range(1, ways):
            rs_copy(z, k).wait_send()
            ag_copy(z, k).wait_send()
        for k in range(1, n_far):
            ar_copy(z, k).wait_send()
            if paired:
                tot_copy(z, k).wait_send()


def finish(src, out, sem):
    copy = pltpu.make_async_copy(src, out, sem)
    copy.start()
    copy.wait()


def body(n_rows, n_cols, tokens, qkv_weight, depth_kernel, group_kernel, proj_weight, out_gain, out_bias):
    height, breadth, d = tokens.shape
    paired = is_paired(n_rows, n_cols, d)
    ways, far = (2, n_rows * n_cols // 2) if paired else (n_cols, n_rows)
    block = (ROWS, PACK) if paired else (ROWS // n_cols, d)
    far_block, far_type = ((HEAD_DIM, PACK), BF) if paired else (block, F32)
    most = 4 * max(ways + far - 2, 1)
    operands = (
        tokens, qkv_weight, depth_kernel, jnp.transpose(group_kernel, (1, 2, 0)), proj_weight, out_gain[None, :], out_bias[None, :])
    operands = [pltpu.with_memory_space_constraint(x, pltpu.HBM) for x in operands]
    mixed = pl.pallas_call(
        functools.partial(kernel, n_rows, n_cols),
        out_shape=pltpu.VMEM((height, breadth, d), BF),
        in_specs=[pl.BlockSpec(memory_space=pl.ANY)] * 7,
        out_specs=pl.BlockSpec(memory_space=pltpu.VMEM),
        scratch_shapes=[pltpu.VMEM(x.shape, x.dtype) for x in operands] + [
            pltpu.VMEM((2, 2 * height, d), BF),
            pltpu.VMEM((4, SUB, d), BF),
            pltpu.VMEM((2, 2 * height, d), BF),
            pltpu.VMEM((4, SUB, d), BF),
            pltpu.VMEM((2, 2, breadth, d), BF),
            pltpu.VMEM((d, 3 * d), BF),
            pltpu.VMEM((3 * d // LANES, 32, LANES), F32),
            pltpu.VMEM((3 * d, LANES), F32),
            pltpu.VMEM((3 * d // PACK, PACK, PACK), BF),
            pltpu.VMEM((3 * d // LANES, (height + 4) * (breadth + 2 * PAD), LANES), F32),
            pltpu.VMEM((3 * d // LANES, height * breadth, LANES), F32),
            pltpu.VMEM((height * breadth, d), F32),
            pltpu.VMEM((d, d), BF),
            pltpu.VMEM((2, ways, *block), F32),
            pltpu.VMEM((2, ways - 1, *block), F32),
            pltpu.VMEM((2, *far_block), far_type),
            pltpu.VMEM((2, far - 1, *far_block), far_type),
            pltpu.VMEM((2, 1, PACK), F32),
            pltpu.VMEM((2, far - 1, 1, PACK), F32),
            pltpu.VMEM((2, ways, *block), F32),
            pltpu.SemaphoreType.DMA((8,)),
            pltpu.SemaphoreType.DMA((8,)),
            pltpu.SemaphoreType.DMA((most,)),
            pltpu.SemaphoreType.DMA((most,)),
            pltpu.SemaphoreType.DMA((7,)),
        ],
        compiler_params=pltpu.CompilerParams(
            collective_id=0, has_side_effects=True, vmem_limit_bytes=48 * 1024 * 1024
        ),
        name="attention_module",
    )(*operands)
    return pl.pallas_call(
        finish,
        out_shape=jax.ShapeDtypeStruct((height, breadth, d), BF),
        in_specs=[pl.BlockSpec(memory_space=pl.ANY)],
        out_specs=pl.BlockSpec(memory_space=pl.ANY),
        scratch_shapes=[pltpu.SemaphoreType.DMA],
        compiler_params=pltpu.CompilerParams(vmem_limit_bytes=4 * 1024 * 1024),
        name="finish",
    )(mixed)


def solution(mesh):
    placed = (P(("groups", "rows"), "cols", None), P(), P(), P(), P(), P(), P())
    return jax.shard_map(
        functools.partial(body, mesh.shape["rows"], mesh.shape["cols"]),
        mesh=mesh,
        in_specs=placed,
        out_specs=P(("groups", "rows"), "cols", None),
        check_vma=False,
    )
```
